512 devices in a mesh: gz: 64 (over y, z_hi, x, core), gy: 8 (over z_lo).
Axes of the slice: x: 4, y: 4, z: 16 (z_hi: 2, z_lo: 8; z = z_hi * 8 + z_lo), core: 2. Of those that a mesh axis runs over, the one named last changes fastest.
Arguments:
- probe_fields: float32 [1, 128, 1024, 1024], P(None, 'gz', 'gy'), may hold values from -24 to 24
- root_one: float32 [128, 1024], P('gz'), may hold values from 0.5 to 0.999
- root_two: float32 [128, 1024], P('gz'), may hold values from 0.3 to 0.8
- lateral_kernel_taps: float32 [2, 3], replicated, may hold values from 0.2 to 1
- dilations: int32 [2], replicated, may hold values from 1 to 8, as said below
Outputs:
- covariance_image: float32 [1, 128, 1024, 1024], P(None, 'gz', 'gy')
The draws below stay inside these ranges and needn't reach their ends.
Inputs may be any that keep to these rules, and one draw needn't show every extreme that they name: `dilations`: one entry equals 8 and the other is smaller.
All inputs are finite; a program needn't handle non-finite values.
Results may differ from the reference program's by a relative error of at most 0.000044.
Values sent between devices are 32-bit elements; how exact they have to be, the bound alone decides.
A program may use at most 64 MiB of HBM per device.

```python
import math
import jax
import jax.numpy as jnp
from jax import lax

PROBES = 1
NX = 1024
RADIUS = 2
DMAX = 8
DEPTH_PLANES = 128
NY = 1024


def draw_root_one(key, part):
    key_base = jax.random.fold_in(key, 11)
    key_jitter = jax.random.fold_in(key, 12)
    random_key_group = jax.random.fold_in(key, 13)
    base = jnp.exp(jax.random.uniform(key_base, (NX,), jnp.float32, math.log(0.003), math.log(0.08)))
    jitter = jnp.exp(jax.random.uniform(key_jitter, (DEPTH_PLANES, NX), jnp.float32, math.log(0.7), math.log(1.4)))
    roots = 1.0 - base[None, :] * jitter
    position_slots = jax.random.randint(random_key_group, (3,), 0, DEPTH_PLANES)
    planes = jnp.arange(DEPTH_PLANES)
    hit = jnp.any(planes[:, None] == position_slots[None, :], axis=1)
    roots = jnp.where(hit[:, None], roots * 0.6, roots)
    return roots.astype(jnp.float32)


def draw_dilations(key, part):
    other = jax.random.randint(jax.random.fold_in(key, 21), (), 1, DMAX)
    which = jax.random.randint(jax.random.fold_in(key, 22), (), 0, 2)
    slots = jnp.arange(2)
    return jnp.where(slots == which, DMAX, other).astype(jnp.int32)


def steps_of(own_key, shape, pieces, low, top_value):
    level, own = 1.0, jax.random.fold_in(own_key, 6)
    for axis_at, blocks in pieces:
        draws = jnp.exp(jax.random.uniform(jax.random.fold_in(own, axis_at), (blocks,), jnp.float32, low / len(pieces), top_value / len(pieces)))
        level = level * jnp.repeat(draws, shape[axis_at] // blocks).reshape([-1 if axis == axis_at else 1 for axis in range(len(shape))])
    return level


def bell_draw(own_key, extent, width, most, split=(), held_as=jnp.bfloat16):
    level = steps_of(own_key, extent, split, -0.22, 0.18) if split else 1.0
    array = jax.random.normal(own_key, extent, jnp.float32) * width * level
    return jnp.minimum(jnp.maximum(array, -most), most).astype(held_as)


def setup_inputs(seed: int = 0) -> dict:
    keys = jax.random.split(jax.random.key(seed), 6)
    probe_fields = bell_draw(keys[0], (PROBES, DEPTH_PLANES, NY, NX), 4.0, 24.0, ((1, 64), (2, 8)), jnp.float32)
    root_one = draw_root_one(jax.random.fold_in(keys[5], 71), 0)
    root_two = jnp.clip(0.3 + 0.5 * jax.random.uniform(keys[2], (DEPTH_PLANES, NX), jnp.float32) ** steps_of(keys[2], (DEPTH_PLANES, NX), ((0, 64),), -0.2, 0.2), 0.3, 0.8)
    lateral_kernel_taps = jnp.clip(jnp.exp(jax.random.uniform(keys[3], (2, RADIUS + 1), jnp.float32, math.log(0.2), math.log(1.0))), 0.2, 1.0)
    dilations = draw_dilations(jax.random.fold_in(keys[5], 71), 0)
    return dict(probe_fields=probe_fields, root_one=root_one, root_two=root_two, lateral_kernel_taps=lateral_kernel_taps, dilations=dilations)


def filter_coefficients(root_one, root_two):
    first = root_one + root_two
    second = -root_one * root_two
    gain = (1.0 - root_one) * (1.0 - root_two)
    return first, second, gain


def adjoint_coefficients(first, second):
    first_next = jnp.concatenate([first[1:], jnp.zeros_like(first[:1])], 0)
    second_next = jnp.concatenate([second[2:], jnp.zeros_like(second[:2])], 0)
    return first_next, second_next


def depth_scan(fields, first, second, pre_gain, post_gain, reverse):
    moved = jnp.moveaxis(fields, 1, 0)
    zero = jnp.zeros(moved.shape[1:], jnp.float32)

    def advance(carry, inputs):
        latest, earlier = carry
        plane, coef_one, coef_two, before, after = inputs
        value = before * plane + coef_one * latest + coef_two * earlier
        return (value, latest), after * value

    _, outputs = lax.scan(advance, (zero, zero), (moved, first, second, pre_gain, post_gain), reverse=reverse)
    return jnp.moveaxis(outputs, 0, 1)


def lateral_padded(padded, weights, dilation, axis, margin, length):
    total = weights[0] + 2.0 * jnp.sum(weights[1:])
    scaled = weights / total
    result = scaled[0] * lax.dynamic_slice_in_dim(padded, margin, length, axis)
    for offset_tap in range(1, weights.shape[0]):
        offset = dilation * offset_tap
        upper = lax.dynamic_slice_in_dim(padded, margin + offset, length, axis)
        lower = lax.dynamic_slice_in_dim(padded, margin - offset, length, axis)
        result = result + scaled[offset_tap] * (upper + lower)
    return result


def lateral(fields, weights, dilation, axis):
    margin = RADIUS * DMAX
    widths = [(0, 0)] * fields.ndim
    widths[axis] = (margin, margin)
    padded = jnp.pad(fields, widths)
    return lateral_padded(padded, weights, dilation, axis, margin, fields.shape[axis])


def reference(probe_fields, root_one, root_two, lateral_kernel_taps, dilations):
    first, second, gain = filter_coefficients(root_one, root_two)
    unity = jnp.ones_like(gain)
    first_next, second_next = adjoint_coefficients(first, second)
    field = depth_scan(probe_fields, first_next, second_next, unity, gain, True)
    field = lateral(field, lateral_kernel_taps[0], dilations[0], 3)
    field = lateral(field, lateral_kernel_taps[1], dilations[1], 2)
    field = lateral(field, lateral_kernel_taps[1], dilations[1], 2)
    field = lateral(field, lateral_kernel_taps[0], dilations[0], 3)
    return depth_scan(field, first, second, gain, unity, False)
```

```python
import functools
import jax
import jax.numpy as jnp
from jax import lax
from jax.experimental import pallas as pl
from jax.experimental.pallas import tpu as pltpu
from jax.sharding import PartitionSpec as P

MESH = pl.DeviceIdType.MESH
F32 = jnp.float32
BF16 = jnp.bfloat16
SIZES = (4, 2, 4, 2)
MARGIN = 16
QUARTERS = 4


def pieces(a):
    high = a.astype(BF16)
    return high, (a - high.astype(F32)).astype(BF16)


def dot3(a, b):
    (ah, al), (bh, bl) = a, b
    dot = functools.partial(jnp.dot, preferred_element_type=F32)
    return dot(ah, bh) + (dot(ah, bl) + dot(al, bh))


def band(shape, shift, taps, row, step):
    i = lax.broadcasted_iota(jnp.int32, shape, 0)
    j = lax.broadcasted_iota(jnp.int32, shape, 1)
    away = jnp.abs(i - j + shift)
    centre, near, far = taps[row, 0], taps[row, 1], taps[row, 2]
    weight = jnp.where(away == 0, centre, 0.0)
    weight = jnp.where(away == step, near, weight)
    weight = jnp.where(away == 2 * step, far, weight)
    return weight / (centre + 2.0 * (near + far))


def kernel(
    sizes, n_slabs, x_ref, one_ref, two_ref, taps, dils, o_ref,
    send, recv, back, roots_s, roots_r, first, second, gain, above, below,
    kx_high, kx_low, trans, spread, ends, starts, ends2, starts2,
    root_sem, halo_sem, out_sem, in_sem, trans_sem, end_sem, end2_sem, home_s, home_r,
):
    ny, nz, nxx, nc = sizes
    group = ny * nxx * nc
    block = nxx * nc * 2
    rows = recv.shape[3]
    g, gy = lax.axis_index("gz"), lax.axis_index("gy")
    core, col = lax.rem(g, nc), lax.rem(g // nc, nxx)
    half, line = lax.rem(g // (nc * nxx), nz), g // (nc * nxx * nz)
    me = (line * nxx + col) * nc + core
    partner = ((line * nz + (1 - half)) * nxx + col) * nc + core

    def reach(n, step):
        return min(step, n - step)

    steps = [(a, b, c) for a in range(ny) for b in range(nxx) for c in range(nc)][1:]
    steps.sort(key=lambda s: (-reach(ny, s[0]) - reach(nxx, s[1]), -min(s[0], 1) - min(s[1], 1)))

    def peers():
        for a, b, c in steps:
            yy, xx, cc = lax.rem(line + a, ny), lax.rem(col + b, nxx), lax.rem(core + c, nc)
            yield ((yy * nz + half) * nxx + xx) * nc + cc, (yy * nxx + xx) * nc + cc

    def remote(src, dst, s, r, gz, slab=gy):
        return pltpu.make_async_remote_copy(
            src, dst, s, r, device_id=(gz, slab), device_id_type=MESH
        )

    def arrived(ref, sem):
        pltpu.make_async_copy(ref, ref, sem).wait()

    has_up, has_down = gy > 0, gy < n_slabs - 1

    barrier = pltpu.get_barrier_semaphore()

    def hello(gz, slab):
        pl.semaphore_signal(barrier, inc=1, device_id=(gz, slab), device_id_type=MESH)

    hello(partner, gy)

    @pl.when(has_up)
    def _():
        hello(g, gy - 1)

    @pl.when(has_down)
    def _():
        hello(g, gy + 1)

    for gz, _ in peers():
        hello(gz, gy)

    for p in range(2):
        for q in range(QUARTERS):
            lanes = slice(256 * q, 256 * q + 256)
            roots_s[p, q : q + 1, :] = one_ref[p : p + 1, lanes]
            roots_s[p, 4 + q : 5 + q, :] = two_ref[p : p + 1, lanes]

    def to_quarters(c, p, at, value):
        n = value.shape[0]
        for q in range(QUARTERS):
            for h in range(2):
                lanes = slice(256 * q + 128 * h, 256 * q + 128 * h + 128)
                send[c, p, h, pl.ds(at * QUARTERS + q, n, stride=QUARTERS), :] = value[:, lanes]

    ky = functools.partial(band, taps=taps, row=1, step=dils[1])
    exact = functools.partial(jnp.dot, precision=lax.Precision.HIGHEST, preferred_element_type=F32)
    inner = pieces(exact(ky((64, 96), MARGIN), ky((96, 128), MARGIN)))
    for p in range(2):
        to_quarters(0, p, 0, dot3(inner, pieces(x_ref[p])))

    pl.semaphore_wait(
        barrier, group + has_up.astype(jnp.int32) + has_down.astype(jnp.int32)
    )

    up = remote(x_ref.at[:, 0:32], below, halo_sem.at[0], halo_sem.at[2], g, gy - 1)
    down = remote(x_ref.at[:, 96:128], above, halo_sem.at[1], halo_sem.at[3], g, gy + 1)

    @pl.when(has_up)
    def _():
        up.start()

    @pl.when(has_down)
    def _():
        down.start()

    for gz, _ in peers():
        remote(roots_s, roots_r.at[pl.ds(2 * me, 2)], root_sem.at[0], root_sem.at[1], gz).start()

    def spread_rows(c):
        for gz, place in peers():
            remote(
                send.at[c, :, :, pl.ds(pl.multiple_of(place * rows, 8), rows)],
                recv.at[c, pl.ds(2 * me, 2)],
                out_sem.at[c], in_sem.at[c], gz,
            ).start()

        recv[c, pl.ds(2 * me, 2)] = send[c, :, :, pl.ds(pl.multiple_of(me * rows, 8), rows)]

    spread_rows(0)
    roots_r[pl.ds(2 * me, 2)] = roots_s[...]
    kx = band((512, 256), -128, taps, 0, dils[0])
    kx_high[...], kx_low[...] = pieces(kx)

    arrived(roots_r.at[pl.ds(0, 2 * group - 2)], root_sem.at[1])
    sub = lax.broadcasted_iota(jnp.int32, (8, 256), 0)

    @pl.loop(0, 2 * group)
    def _(k):
        both = roots_r[k]
        turned = pltpu.roll(both, 4, 0)
        one, two = jnp.where(sub < 4, both, turned), jnp.where(sub < 4, turned, both)
        first[k], second[k] = one + two, -one * two
        gain[k] = (1.0 - one) * (1.0 - two)

    def advance(k, states):
        out = []
        for b, (y1, y2) in enumerate(states):
            at = b * block + k
            out.append((first[at] * y1 + second[at] * y2, y1))
        return tuple(out)

    unit = (jnp.where(sub < 4, 1.0, 0.0), jnp.where(sub < 4, 0.0, 1.0))
    done = advance(1, advance(0, [unit] * ny))
    done = lax.fori_loop(2, block, advance, done)
    for b, (y1, y2) in enumerate(done):
        trans[half, b, 0] = y1
        trans[half, b, 1] = y2
    trans_copy = remote(trans.at[half], trans.at[half], trans_sem.at[0], trans_sem.at[1], partner)
    trans_copy.start()

    @pl.when(has_up)
    def _():
        down.wait_recv()

    @pl.when(jnp.logical_not(has_up))
    def _():
        above[...] = jnp.zeros_like(above)

    @pl.when(has_down)
    def _():
        up.wait_recv()

    @pl.when(jnp.logical_not(has_down))
    def _():
        below[...] = jnp.zeros_like(below)

    mid = lax.broadcasted_iota(jnp.int32, (64, 96), 0)
    head, tail = ky((32, 64), MARGIN), ky((64, 96), MARGIN)
    top = pieces(exact(head, jnp.where(has_up | (mid >= MARGIN), tail, 0.0)))
    bottom = pieces(exact(head, jnp.where(has_down | (mid < 64 - MARGIN), tail, 0.0)))
    for p in range(2):
        over = jnp.concatenate([above[p], x_ref[p, 0:64]], 0)
        to_quarters(1, p, 0, dot3(top, pieces(over)))
        under = jnp.concatenate([x_ref[p, 64:128], below[p]], 0)
        to_quarters(1, p, 32, dot3(bottom, pieces(under)))
    spread_rows(1)

    def load(c, k):
        return jnp.concatenate([recv[c, k, 0], recv[c, k, 1]], -1)

    def store(c, k, value):
        recv[c, k, 0] = value[:, :128]
        recv[c, k, 1] = value[:, 128:]

    def back_scan(c, begin, keep):
        def step(i, states):
            out = []
            for b, (u, t) in enumerate(states):
                at = b * block + block - 1 - i
                z = load(c, at) + u
                if keep:
                    store(c, at, gain[at] * z)
                out.append((first[at] * z + t, second[at] * z))
            return tuple(out)

        return lax.fori_loop(2, block, step, step(1, step(0, begin)))

    def fore_scan(c, begin, keep):
        def step(k, states):
            out = []
            for b, (y1, y2) in enumerate(states):
                at = b * block + k
                y = gain[at] * load(c, at) + first[at] * y1 + second[at] * y2
                if keep:
                    store(c, at, y)
                out.append((y, y1))
            return tuple(out)

        return lax.fori_loop(2, block, step, step(1, step(0, begin)))

    zero = jnp.zeros((rows, 256), F32)
    nothing = [(zero, zero)] * ny

    def hand_over(buf, sems, c, states):
        for b, (s1, s2) in enumerate(states):
            buf[c, half, b, 0] = s1
            buf[c, half, b, 1] = s2
        remote(
            buf.at[c, half], buf.at[c, half], sems.at[0, c], sems.at[1, c], partner
        ).start()

    def x_twice(c):
        @pl.loop(0, ny)
        def _(b):
            n = block * rows
            quarter = lax.rem(lax.broadcasted_iota(jnp.int32, (n, 128), 0), QUARTERS)
            at = pl.ds(b * block, block)
            left = recv[c, at, 0].reshape(n, 128)
            right = recv[c, at, 1].reshape(n, 128)
            matrix = (kx_high[...], kx_low[...])
            for _ in range(2):
                before = jnp.where(quarter == 0, 0.0, pltpu.roll(right, 1, 0))
                after = jnp.where(quarter == 3, 0.0, pltpu.roll(left, n - 1, 0))
                whole = dot3(pieces(jnp.concatenate([before, left, right, after], 1)), matrix)
                left, right = whole[:, :128], whole[:, 128:]
            recv[c, at, 0] = left.reshape(block, rows, 128)
            recv[c, at, 1] = right.reshape(block, rows, 128)

    for c in range(2):
        arrived(recv.at[c, pl.ds(0, 2 * group - 2)], in_sem.at[c])
        hand_over(ends, end_sem, c, back_scan(c, nothing, False))

    trans_copy.wait_recv()
    for z in range(nz):
        for b in range(ny):
            for s in range(2):
                a = trans[z, b, s]
                turned = pltpu.roll(a, 4, 0)
                spread[z, b, s, 0] = jnp.where(sub < 4, a, turned)
                spread[z, b, s, 1] = jnp.where(sub < 4, turned, a)

    for c in range(2):
        arrived(ends.at[c, 1 - half], end_sem.at[1, c])
        u, t = zero, zero
        for j in reversed(range(ny * nz)):
            b, z = j // nz, j % nz
            starts[c, z, b, 0], starts[c, z, b, 1] = u, t
            u, t = (
                spread[z, b, 0, 0] * u + spread[z, b, 1, 0] * t + ends[c, z, b, 0],
                spread[z, b, 0, 1] * u + spread[z, b, 1, 1] * t + ends[c, z, b, 1],
            )
        begin = [(starts[c, half, b, 0], starts[c, half, b, 1]) for b in range(ny)]
        back_scan(c, begin, True)
        x_twice(c)
        hand_over(ends2, end2_sem, c, fore_scan(c, nothing, False))

    for c in range(2):
        arrived(ends2.at[c, 1 - half], end2_sem.at[1, c])
        y1, y2 = zero, zero
        for j in range(ny * nz):
            b, z = j // nz, j % nz
            starts2[c, z, b, 0], starts2[c, z, b, 1] = y1, y2
            y1, y2 = (
                spread[z, b, 0, 0] * y1 + spread[z, b, 0, 1] * y2 + ends2[c, z, b, 0],
                spread[z, b, 1, 0] * y1 + spread[z, b, 1, 1] * y2 + ends2[c, z, b, 1],
            )
        begin = [(starts2[c, half, b, 0], starts2[c, half, b, 1]) for b in range(ny)]
        fore_scan(c, begin, True)

        for gz, place in peers():
            remote(
                recv.at[c, pl.ds(2 * place, 2)],
                back.at[c, :, :, pl.ds(pl.multiple_of(me * rows, 8), rows)],
                home_s.at[c], home_r.at[c], gz,
            ).start()

        back[c, :, :, pl.ds(pl.multiple_of(me * rows, 8), rows)] = recv[c, pl.ds(2 * me, 2)]

    for c in range(2):
        arrived(back.at[c, :, :, pl.ds(0, (group - 1) * rows)], home_r.at[c])
        for p in range(2):
            for q in range(QUARTERS):
                for h in range(2):
                    lanes = slice(256 * q + 128 * h, 256 * q + 128 * h + 128)
                    for at, to, n in ((0, 32, 64),) if c == 0 else ((0, 0, 32), (32, 96, 32)):
                        o_ref[p, to : to + n, lanes] = back[
                            c, p, h, pl.ds(at * QUARTERS + q, n, stride=QUARTERS), :
                        ]

    @pl.when(has_up)
    def _():
        up.wait_send()

    @pl.when(has_down)
    def _():
        down.wait_send()

    trans_copy.wait_send()
    arrived(roots_r.at[pl.ds(0, 2 * group - 2)], root_sem.at[0])
    for c in range(2):
        arrived(send.at[c, :, :, pl.ds(0, (group - 1) * rows)], out_sem.at[c])
        arrived(ends.at[c, 0], end_sem.at[0, c])
        arrived(ends2.at[c, 0], end2_sem.at[0, c])
        arrived(back.at[c, :, :, pl.ds(0, (group - 1) * rows)], home_s.at[c])


def build(sizes, n_slabs):
    ny, nz, nxx, nc = sizes
    group = ny * nxx * nc
    rows = 64 // group * QUARTERS

    def body(probe_fields, root_one, root_two, lateral_kernel_taps, dilations):
        vmem, smem = (pl.BlockSpec(memory_space=s) for s in (pltpu.VMEM, pltpu.SMEM))
        dma = pltpu.SemaphoreType.DMA
        out = pl.pallas_call(
            functools.partial(kernel, sizes, n_slabs),
            out_shape=jax.ShapeDtypeStruct((2, 128, 1024), F32),
            in_specs=[vmem, vmem, vmem, smem, smem],
            out_specs=vmem,
            scratch_shapes=[
                pltpu.VMEM((2, 2, 2, 256, 128), F32),
                pltpu.VMEM((2, 2 * group, 2, rows, 128), F32),
                pltpu.VMEM((2, 2, 2, 256, 128), F32),
                pltpu.VMEM((2, 8, 256), F32),
                pltpu.VMEM((2 * group, 8, 256), F32),
                pltpu.VMEM((2 * group, 8, 256), F32),
                pltpu.VMEM((2 * group, 8, 256), F32),
                pltpu.VMEM((2 * group, 8, 256), F32),
                pltpu.VMEM((2, 32, 1024), F32),
                pltpu.VMEM((2, 32, 1024), F32),
                pltpu.VMEM((512, 256), BF16),
                pltpu.VMEM((512, 256), BF16),
                pltpu.VMEM((nz, ny, 2, 8, 256), F32),
                pltpu.VMEM((nz, ny, 2, 2, 8, 256), F32),
                pltpu.VMEM((2, nz, ny, 2, rows, 256), F32),
                pltpu.VMEM((2, nz, ny, 2, rows, 256), F32),
                pltpu.VMEM((2, nz, ny, 2, rows, 256), F32),
                pltpu.VMEM((2, nz, ny, 2, rows, 256), F32),
                dma((2,)),
                dma((4,)),
                dma((2,)),
                dma((2,)),
                dma((2,)),
                dma((2, 2)),
                dma((2, 2)),
                dma((2,)),
                dma((2,)),
            ],
            compiler_params=pltpu.CompilerParams(
                collective_id=0, has_side_effects=True, vmem_limit_bytes=48 << 20
            ),
        )(probe_fields[0], root_one, root_two, lateral_kernel_taps, dilations)
        return out[None]

    return body


def solution(mesh):
    placed = (P(None, "gz", "gy", None), P("gz", None), P("gz", None), P(), P())
    return jax.shard_map(
        build(SIZES, mesh.shape["gy"]),
        mesh=mesh,
        in_specs=placed,
        out_specs=P(None, "gz", "gy", None),
        check_vma=False,
    )
```

```python
import functools
import jax
import jax.numpy as jnp
from jax import lax
from jax.experimental import pallas as pl
from jax.experimental.pallas import tpu as pltpu
from jax.sharding import PartitionSpec as P

MESH = pl.DeviceIdType.MESH
F32 = jnp.float32
BF16 = jnp.bfloat16
SIZES = (4, 2, 4, 2)
MARGIN = 16
EIGHTHS = 8
RUNS = (32, 64, 0, 96)
CHUNKS = ((0, 1), (1, 1), (2, 1), (3, 1))


def pieces(a):
    high = a.astype(BF16)
    return high, (a - high.astype(F32)).astype(BF16)


def dot3(a, b):
    (ah, al), (bh, bl) = a, b
    dot = functools.partial(jnp.dot, preferred_element_type=F32)
    return dot(ah, bh) + (dot(ah, bl) + dot(al, bh))


def stencil(away, taps, row, step):
    centre, near, far = taps[row, 0], taps[row, 1], taps[row, 2]
    weight = jnp.where(away == 0, centre, 0.0)
    weight = jnp.where(away == step, near, weight)
    weight = jnp.where(away == 2 * step, far, weight)
    return weight / (centre + 2.0 * (near + far))


def kernel(
    sizes, n_slabs, x_hbm, one_hbm, two_hbm, taps_hbm, dils_hbm, o_ref,
    x_ref, one_ref, two_ref, taps, dils, send, recv, back, roots_s, roots_r, first, second, gain,
    above, below, kx_high, kx_low, trans, ends, ends2, starts,
    load_sem, root_sem, halo_sem, out_sem, in_sem, trans_sem, end_sem, end2_sem, home_s, home_r,
):
    ny, nz, nxx, nc = sizes
    chips = ny * nxx
    group = chips * nc
    block = nxx * nc * 2
    g, gy = lax.axis_index("gz"), lax.axis_index("gy")
    core, col = lax.rem(g, nc), lax.rem(g // nc, nxx)
    half, line = lax.rem(g // (nc * nxx), nz), g // (nc * nxx * nz)
    chip = line * nxx + col
    me = chip * nc + core

    def gz_of(yy, zz, xx, cc):
        return ((yy * nz + zz) * nxx + xx) * nc + cc

    partner, sibling = gz_of(line, 1 - half, col, core), gz_of(line, half, col, 1 - core)

    def reach(n, step):
        return min(step, n - step)

    steps = [(a, b, c) for a in range(ny) for b in range(nxx) for c in range(nc)][1:]
    steps.sort(key=lambda s: (-reach(ny, s[0]) - reach(nxx, s[1]), -min(s[0], 1) - min(s[1], 1)))

    def peers(same_core=False):
        for a, b, c in steps:
            if same_core and c:
                continue
            yy, xx, cc = lax.rem(line + a, ny), lax.rem(col + b, nxx), lax.rem(core + c, nc)
            yield gz_of(yy, half, xx, cc), (yy * nxx + xx) * nc + cc

    def remote(src, dst, s, r, gz, slab=gy):
        return pltpu.make_async_remote_copy(
            src, dst, s, r, device_id=(gz, slab), device_id_type=MESH
        )

    def arrived(ref, sem):
        pltpu.make_async_copy(ref, ref, sem).wait()

    def flat(place):
        return pl.ds(pl.multiple_of(place * EIGHTHS, EIGHTHS), EIGHTHS)

    loads = [
        pltpu.make_async_copy(a, b, load_sem.at[i])
        for i, (a, b) in enumerate(
            (
                (one_hbm, one_ref),
                (two_hbm, two_ref),
                (taps_hbm, taps),
                (dils_hbm, dils),
                (x_hbm, x_ref),
            )
        )
    ]
    for copy in loads:
        copy.start()

    has_up, has_down = gy > 0, gy < n_slabs - 1

    barrier = pltpu.get_barrier_semaphore()

    def hello(gz, slab):
        pl.semaphore_signal(barrier, inc=1, device_id=(gz, slab), device_id_type=MESH)

    hello(partner, gy)

    @pl.when(has_up)
    def _():
        hello(g, gy - 1)

    @pl.when(has_down)
    def _():
        hello(g, gy + 1)

    for gz, _ in peers():
        hello(gz, gy)

    loads[0].wait()
    loads[1].wait()
    for p in range(2):
        for e in range(EIGHTHS):
            lanes = slice(128 * e, 128 * e + 128)
            roots_s[p, 0, e : e + 1, :] = one_ref[p : p + 1, lanes]
            roots_s[p, 1, e : e + 1, :] = two_ref[p : p + 1, lanes]

    loads[2].wait()
    loads[3].wait()
    exact = functools.partial(jnp.dot, precision=lax.Precision.HIGHEST, preferred_element_type=F32)

    def ky(n_out, n_in):
        i = lax.broadcasted_iota(jnp.int32, (n_out, n_in), 0)
        j = lax.broadcasted_iota(jnp.int32, (n_out, n_in), 1)
        return stencil(jnp.abs(i - j + MARGIN), taps, 1, dils[1])

    def to_flat(slot, p, value):
        for e in range(EIGHTHS):
            send[slot, p, pl.ds(e, 32, stride=EIGHTHS), :] = value[:, 128 * e : 128 * e + 128]

    inner = pieces(exact(ky(64, 96), ky(96, 128)))
    loads[4].wait()
    for p in range(2):
        middle = dot3(inner, pieces(x_ref[p]))
        to_flat(0, p, middle[:32])
        to_flat(1, p, middle[32:])

    pl.semaphore_wait(
        barrier, group + has_up.astype(jnp.int32) + has_down.astype(jnp.int32)
    )

    for gz, _ in peers(True):
        remote(roots_s, roots_r.at[core, chip], root_sem.at[0], root_sem.at[1], gz).start()
    up = remote(x_ref.at[:, 0:32], below, halo_sem.at[0], halo_sem.at[2], g, gy - 1)
    down = remote(x_ref.at[:, 96:128], above, halo_sem.at[1], halo_sem.at[3], g, gy + 1)

    @pl.when(has_up)
    def _():
        up.start()

    @pl.when(has_down)
    def _():
        down.start()

    def spread_rows(n):
        at = pl.ds(*CHUNKS[n])
        for gz, place in peers():
            remote(
                send.at[at, :, flat(place)], recv.at[at, pl.ds(2 * me, 2)],
                out_sem.at[n], in_sem.at[n], gz,
            ).start()
        recv[at, pl.ds(2 * me, 2)] = send[at, :, flat(me)]

    inner_chunks = [n for n, (s, _) in enumerate(CHUNKS) if s < 2]
    outer_chunks = [n for n, (s, _) in enumerate(CHUNKS) if s >= 2]
    for n in inner_chunks:
        spread_rows(n)
    roots_r[core, chip] = roots_s[...]

    i = lax.broadcasted_iota(jnp.int32, (256, 128), 0)
    j = lax.broadcasted_iota(jnp.int32, (256, 128), 1)
    kx = stencil(jnp.abs(jnp.where(i < 192, i, i - 256) - j), taps, 0, dils[0])
    kx_high[...], kx_low[...] = pieces(kx)

    arrived(roots_r.at[0, pl.ds(0, chips - 1)], root_sem.at[1])
    root_copy = remote(
        roots_r.at[core], roots_r.at[core], root_sem.at[2], root_sem.at[3], sibling
    )
    root_copy.start()

    head, tail = ky(32, 64), ky(64, 96)
    mid = lax.broadcasted_iota(jnp.int32, (64, 96), 0)
    top = pieces(exact(head, jnp.where(has_up | (mid >= MARGIN), tail, 0.0)))
    bottom = pieces(exact(head, jnp.where(has_down | (mid < 64 - MARGIN), tail, 0.0)))

    root_copy.wait_recv()

    @pl.loop(0, 2 * group)
    def _(k):
        c, ch, p = lax.rem(k // 2, nc), k // (2 * nc), lax.rem(k, 2)
        one, two = roots_r[c, ch, p, 0], roots_r[c, ch, p, 1]
        first[k], second[k] = one + two, -one * two
        gain[k] = (1.0 - one) * (1.0 - two)

    def advance(k, states):
        out = []
        for b in range(ny):
            at = b * block + k
            f, s = first[at], second[at]
            out.append(tuple((f * y1 + s * y2, y1) for y1, y2 in states[b]))
        return tuple(out)

    begin = []
    for b in range(ny):
        f0, s0, f1, s1 = first[b * block], second[b * block], first[b * block + 1], second[b * block + 1]
        begin.append(((f1 * f0 + s1, f0), (f1 * s0, s0)))
    done = lax.fori_loop(2, block, advance, tuple(begin))
    for b in range(ny):
        (a, c), (d, e) = done[b]
        for n, value in enumerate((a, d, c, e)):
            trans[half, 4 * b + n] = value
    trans_copy = remote(
        trans.at[half, chip], trans.at[half, chip], trans_sem.at[0], trans_sem.at[1], partner
    )
    trans_copy.start()

    @pl.when(has_up)
    def _():
        down.wait_recv()

    @pl.when(jnp.logical_not(has_up))
    def _():
        above[...] = jnp.zeros_like(above)

    @pl.when(has_down)
    def _():
        up.wait_recv()

    @pl.when(jnp.logical_not(has_down))
    def _():
        below[...] = jnp.zeros_like(below)

    for p in range(2):
        over = jnp.concatenate([above[p], x_ref[p, 0:64]], 0)
        to_flat(2, p, dot3(top, pieces(over)))
    for n in outer_chunks[:1]:
        if len(outer_chunks) == 2:
            spread_rows(n)
    for p in range(2):
        under = jnp.concatenate([x_ref[p, 64:128], below[p]], 0)
        to_flat(3, p, dot3(bottom, pieces(under)))
    spread_rows(outer_chunks[-1])

    def back_scan(slot, begin, keep):
        def step(i, states):
            out = []
            for b, (u, t) in enumerate(states):
                at = b * block + block - 1 - i
                z = recv[slot, at] + u
                if keep:
                    recv[slot, at] = gain[at] * z
                out.append((first[at] * z + t, second[at] * z))
            return tuple(out)

        return lax.fori_loop(2, block, step, step(1, step(0, begin)))

    def fore_scan(slot, begin, keep):
        def step(k, states):
            out = []
            for b, (y1, y2) in enumerate(states):
                at = b * block + k
                y = gain[at] * recv[slot, at] + first[at] * y1 + second[at] * y2
                if keep:
                    recv[slot, at] = y
                out.append((y, y1))
            return tuple(out)

        return lax.fori_loop(2, block, step, step(1, step(0, begin)))

    zero = jnp.zeros((EIGHTHS, 128), F32)
    nothing = [(zero, zero)] * ny

    def slots(n):
        return range(CHUNKS[n][0], sum(CHUNKS[n]))

    def hand_over(buf, sems, n, scan):
        for slot in slots(n):
            for b, (s1, s2) in enumerate(scan(slot, nothing, False)):
                buf[slot, half, b, 0] = s1
                buf[slot, half, b, 1] = s2
        at = pl.ds(*CHUNKS[n])
        remote(
            buf.at[at, half], buf.at[at, half], sems.at[0, n], sems.at[1, n], partner
        ).start()

    def x_twice(slot):
        n = 2 * group * EIGHTHS
        eighth = lax.rem(lax.broadcasted_iota(jnp.int32, (n, 128), 0), EIGHTHS)
        lane = lax.broadcasted_iota(jnp.int32, (n, 128), 1)
        own = recv[slot].reshape(n, 128)
        matrix = (kx_high[...], kx_low[...])
        for _ in range(2):
            before = jnp.where(eighth == 0, 0.0, pltpu.roll(own, 1, 0))
            after = jnp.where(eighth == EIGHTHS - 1, 0.0, pltpu.roll(own, n - 1, 0))
            sides = jnp.where(lane < 64, after, before)
            own = dot3(pieces(jnp.concatenate([own, sides], 1)), matrix)
        recv[slot] = own.reshape(2 * group, EIGHTHS, 128)

    def far_state(buf, n):
        arrived(buf.at[pl.ds(*CHUNKS[n]), 1 - half], (end_sem if buf is ends else end2_sem).at[1, n])

    for n in range(len(CHUNKS)):
        arrived(recv.at[pl.ds(*CHUNKS[n]), pl.ds(0, 2 * group - 2)], in_sem.at[n])
        hand_over(ends, end_sem, n, back_scan)
        if n == 0:
            trans_copy.wait_recv()
            for gz, _ in peers(True):
                remote(
                    trans.at[1 - half, chip], trans.at[1 - half, chip],
                    trans_sem.at[2], trans_sem.at[3], gz,
                ).start()

    arrived(trans.at[1 - half, pl.ds(0, chips - 1)], trans_sem.at[3])

    for n in range(len(CHUNKS)):
        far_state(ends, n)
        for slot in slots(n):
            u, t = zero, zero
            for j in reversed(range(ny * nz)):
                b, z = j // nz, j % nz
                starts[slot, z, b, 0], starts[slot, z, b, 1] = u, t
                a11, a12, a21, a22 = (trans[z, 4 * b + i] for i in range(4))
                u, t = a11 * u + a21 * t + ends[slot, z, b, 0], a12 * u + a22 * t + ends[slot, z, b, 1]
            begin = [(starts[slot, half, b, 0], starts[slot, half, b, 1]) for b in range(ny)]
            back_scan(slot, begin, True)
            x_twice(slot)
        hand_over(ends2, end2_sem, n, fore_scan)

    for n in range(len(CHUNKS)):
        far_state(ends2, n)
        for slot in slots(n):
            y1, y2 = zero, zero
            for j in range(ny * nz):
                b, z = j // nz, j % nz
                starts[slot, z, b, 0], starts[slot, z, b, 1] = y1, y2
                a11, a12, a21, a22 = (trans[z, 4 * b + i] for i in range(4))
                y1, y2 = (
                    a11 * y1 + a12 * y2 + ends2[slot, z, b, 0],
                    a21 * y1 + a22 * y2 + ends2[slot, z, b, 1],
                )
            begin = [(starts[slot, half, b, 0], starts[slot, half, b, 1]) for b in range(ny)]
            fore_scan(slot, begin, True)
        at = pl.ds(*CHUNKS[n])
        for gz, place in peers():
            remote(
                recv.at[at, pl.ds(2 * place, 2)], back.at[at, :, flat(me)],
                home_s.at[n], home_r.at[n], gz,
            ).start()
        back[at, :, flat(me)] = recv[at, pl.ds(2 * me, 2)]

    for n in range(len(CHUNKS)):
        arrived(back.at[pl.ds(*CHUNKS[n]), :, pl.ds(0, (group - 1) * EIGHTHS)], home_r.at[n])
        for slot in slots(n):
            to = RUNS[slot]
            for p in range(2):
                for e in range(EIGHTHS):
                    o_ref[p, to : to + 32, 128 * e : 128 * e + 128] = back[
                        slot, p, pl.ds(e, 32, stride=EIGHTHS), :
                    ]

    @pl.when(has_up)
    def _():
        up.wait_send()

    @pl.when(has_down)
    def _():
        down.wait_send()

    trans_copy.wait_send()
    root_copy.wait_send()
    arrived(trans.at[1 - half, pl.ds(0, chips - 1)], trans_sem.at[2])
    arrived(roots_r.at[0, pl.ds(0, chips - 1)], root_sem.at[0])
    for n in range(len(CHUNKS)):
        at = pl.ds(*CHUNKS[n])
        arrived(send.at[at, :, pl.ds(0, (group - 1) * EIGHTHS)], out_sem.at[n])
        arrived(ends.at[at, 0], end_sem.at[0, n])
        arrived(ends2.at[at, 0], end2_sem.at[0, n])
        arrived(back.at[at, :, pl.ds(0, (group - 1) * EIGHTHS)], home_s.at[n])


def build(sizes, n_slabs):
    ny, nz, nxx, nc = sizes
    chips = ny * nxx
    group = chips * nc
    steps = len(CHUNKS)

    def body(probe_fields, root_one, root_two, lateral_kernel_taps, dilations):
        dma, vmem, smem = pltpu.SemaphoreType.DMA, pltpu.VMEM, pltpu.SMEM
        out = pl.pallas_call(
            functools.partial(kernel, sizes, n_slabs),
            out_shape=jax.ShapeDtypeStruct((2, 128, 1024), F32),
            in_specs=[pl.BlockSpec(memory_space=pltpu.HBM)] * 5,
            out_specs=pl.BlockSpec(memory_space=vmem),
            scratch_shapes=[
                vmem((2, 128, 1024), F32),
                vmem((2, 1024), F32),
                vmem((2, 1024), F32),
                smem((2, 3), F32),
                smem((2,), jnp.int32),
                vmem((4, 2, 256, 128), F32),
                vmem((4, 2 * group, 8, 128), F32),
                vmem((4, 2, 256, 128), F32),
                vmem((2, 2, 8, 128), F32),
                vmem((nc, chips, 2, 2, 8, 128), F32),
                vmem((2 * group, 8, 128), F32),
                vmem((2 * group, 8, 128), F32),
                vmem((2 * group, 8, 128), F32),
                vmem((2, 32, 1024), F32),
                vmem((2, 32, 1024), F32),
                vmem((256, 128), BF16),
                vmem((256, 128), BF16),
                vmem((nz, 4 * ny, 8, 128), F32),
                vmem((4, nz, ny, 2, 8, 128), F32),
                vmem((4, nz, ny, 2, 8, 128), F32),
                vmem((4, nz, ny, 2, 8, 128), F32),
                dma((5,)),
                dma((4,)),
                dma((4,)),
                dma((steps,)),
                dma((steps,)),
                dma((4,)),
                dma((2, steps)),
                dma((2, steps)),
                dma((steps,)),
                dma((steps,)),
            ],
            compiler_params=pltpu.CompilerParams(
                collective_id=0, has_side_effects=True, vmem_limit_bytes=48 << 20
            ),
        )(probe_fields[0], root_one, root_two, lateral_kernel_taps, dilations)
        return out[None]

    return body


def solution(mesh):
    placed = (P(None, "gz", "gy", None), P("gz", None), P("gz", None), P(), P())
    return jax.shard_map(
        build(SIZES, mesh.shape["gy"]),
        mesh=mesh,
        in_specs=placed,
        out_specs=P(None, "gz", "gy", None),
        check_vma=False,
    )
```

```python
import functools
import jax
import jax.numpy as jnp
from jax import lax
from jax.experimental import pallas as pl
from jax.experimental.pallas import tpu as pltpu
from jax.sharding import PartitionSpec as P

MESH = pl.DeviceIdType.MESH
F32 = jnp.float32
BF16 = jnp.bfloat16
SIZES = (4, 2, 4, 2)
MARGIN = 16
EIGHTHS = 8
RUNS = (32, 64, 0, 96)
CHUNKS = ((0, 1), (1, 1), (2, 1), (3, 1))


def pieces(a):
    high = a.astype(BF16)
    return high, (a - high.astype(F32)).astype(BF16)


def dot3(a, b):
    (ah, al), (bh, bl) = a, b
    dot = functools.partial(jnp.dot, preferred_element_type=F32)
    return dot(ah, bh) + (dot(ah, bl) + dot(al, bh))


def stencil(away, taps, row, step):
    centre, near, far = taps[row, 0], taps[row, 1], taps[row, 2]
    weight = jnp.where(away == 0, centre, 0.0)
    weight = jnp.where(away == step, near, weight)
    weight = jnp.where(away == 2 * step, far, weight)
    return weight / (centre + 2.0 * (near + far))


def kernel(
    sizes, n_slabs, x_hbm, one_hbm, two_hbm, taps_hbm, dils_hbm, o_ref,
    x_ref, one_ref, two_ref, taps, dils, send, recv, back, roots_s, roots_r, first, second, gain,
    above, below, kx_high, kx_low, trans, ends, ends2, starts,
    load_sem, ready_sem, root_sem, halo_sem, out_sem, in_sem, trans_sem, end_sem, end2_sem, home_s, home_r,
):
    ny, nz, nxx, nc = sizes
    chips = ny * nxx
    group = chips * nc
    block = nxx * nc * 2
    g, gy = lax.axis_index("gz"), lax.axis_index("gy")
    core, col = lax.rem(g, nc), lax.rem(g // nc, nxx)
    half, line = lax.rem(g // (nc * nxx), nz), g // (nc * nxx * nz)
    chip = line * nxx + col
    me = chip * nc + core

    def gz_of(yy, zz, xx, cc):
        return ((yy * nz + zz) * nxx + xx) * nc + cc

    partner, sibling = gz_of(line, 1 - half, col, core), gz_of(line, half, col, 1 - core)

    def reach(n, step):
        return min(step, n - step)

    steps = [(a, b, c) for a in range(ny) for b in range(nxx) for c in range(nc)][1:]
    steps.sort(key=lambda s: (-reach(ny, s[0]) - reach(nxx, s[1]), -min(s[0], 1) - min(s[1], 1)))

    def peers(same_core=False):
        for a, b, c in steps:
            if same_core and c:
                continue
            yy, xx, cc = lax.rem(line + a, ny), lax.rem(col + b, nxx), lax.rem(core + c, nc)
            yield gz_of(yy, half, xx, cc), (yy * nxx + xx) * nc + cc

    def remote(src, dst, s, r, gz, slab=gy):
        return pltpu.make_async_remote_copy(
            src, dst, s, r, device_id=(gz, slab), device_id_type=MESH
        )

    def arrived(ref, sem):
        pltpu.make_async_copy(ref, ref, sem).wait()

    def flat(place):
        return pl.ds(pl.multiple_of(place * EIGHTHS, EIGHTHS), EIGHTHS)

    loads = [
        pltpu.make_async_copy(a, b, load_sem.at[i])
        for i, (a, b) in enumerate(
            (
                (one_hbm, one_ref),
                (two_hbm, two_ref),
                (taps_hbm, taps),
                (dils_hbm, dils),
                (x_hbm, x_ref),
            )
        )
    ]
    for copy in loads:
        copy.start()

    has_up, has_down = gy > 0, gy < n_slabs - 1

    barrier = pltpu.get_barrier_semaphore()

    def hello(gz, slab):
        pl.semaphore_signal(barrier, inc=1, device_id=(gz, slab), device_id_type=MESH)

    leads = half == 0

    @pl.when(leads)
    def _():
        hello(partner, gy)

    @pl.when(has_up)
    def _():
        hello(g, gy - 1)

    @pl.when(has_down)
    def _():
        hello(g, gy + 1)

    for gz, _ in peers():
        hello(gz, gy)

    loads[0].wait()
    loads[1].wait()
    for p in range(2):
        for e in range(EIGHTHS):
            lanes = slice(128 * e, 128 * e + 128)
            roots_s[p, 0, e : e + 1, :] = one_ref[p : p + 1, lanes]
            roots_s[p, 1, e : e + 1, :] = two_ref[p : p + 1, lanes]

    loads[2].wait()
    loads[3].wait()
    exact = functools.partial(jnp.dot, precision=lax.Precision.HIGHEST, preferred_element_type=F32)

    def ky(n_out, n_in):
        i = lax.broadcasted_iota(jnp.int32, (n_out, n_in), 0)
        j = lax.broadcasted_iota(jnp.int32, (n_out, n_in), 1)
        return stencil(jnp.abs(i - j + MARGIN), taps, 1, dils[1])

    def to_flat(slot, p, value):
        for e in range(EIGHTHS):
            send[slot, p, pl.ds(e, 32, stride=EIGHTHS), :] = value[:, 128 * e : 128 * e + 128]

    inner = pieces(exact(ky(64, 96), ky(96, 128)))
    loads[4].wait()
    for p in range(2):
        middle = dot3(inner, pieces(x_ref[p]))
        to_flat(0, p, middle[:32])
        to_flat(1, p, middle[32:])

    pl.semaphore_wait(
        barrier, group - 1 + half + has_up.astype(jnp.int32) + has_down.astype(jnp.int32)
    )

    @pl.when(jnp.logical_not(leads))
    def _():
        pl.semaphore_signal(ready_sem, inc=1, device_id=(partner, gy), device_id_type=MESH)

    for gz, _ in peers(True):
        remote(roots_s, roots_r.at[core, chip], root_sem.at[0], root_sem.at[1], gz).start()
    up = remote(x_ref.at[:, 0:32], below, halo_sem.at[0], halo_sem.at[2], g, gy - 1)
    down = remote(x_ref.at[:, 96:128], above, halo_sem.at[1], halo_sem.at[3], g, gy + 1)

    @pl.when(has_up)
    def _():
        up.start()

    @pl.when(has_down)
    def _():
        down.start()

    def spread_rows(n):
        at = pl.ds(*CHUNKS[n])
        for gz, place in peers():
            remote(
                send.at[at, :, flat(place)], recv.at[at, pl.ds(2 * me, 2)],
                out_sem.at[n], in_sem.at[n], gz,
            ).start()
        recv[at, pl.ds(2 * me, 2)] = send[at, :, flat(me)]

    inner_chunks = [n for n, (s, _) in enumerate(CHUNKS) if s < 2]
    outer_chunks = [n for n, (s, _) in enumerate(CHUNKS) if s >= 2]
    for n in inner_chunks:
        spread_rows(n)
    roots_r[core, chip] = roots_s[...]

    i = lax.broadcasted_iota(jnp.int32, (256, 128), 0)
    j = lax.broadcasted_iota(jnp.int32, (256, 128), 1)
    kx = stencil(jnp.abs(jnp.where(i < 192, i, i - 256) - j), taps, 0, dils[0])
    kx_high[...], kx_low[...] = pieces(kx)

    arrived(roots_r.at[0, pl.ds(0, chips - 1)], root_sem.at[1])
    root_copy = remote(
        roots_r.at[core], roots_r.at[core], root_sem.at[2], root_sem.at[3], sibling
    )
    root_copy.start()

    head, tail = ky(32, 64), ky(64, 96)
    mid = lax.broadcasted_iota(jnp.int32, (64, 96), 0)
    top = pieces(exact(head, jnp.where(has_up | (mid >= MARGIN), tail, 0.0)))
    bottom = pieces(exact(head, jnp.where(has_down | (mid < 64 - MARGIN), tail, 0.0)))

    root_copy.wait_recv()

    @pl.loop(0, 2 * group)
    def _(k):
        c, ch, p = lax.rem(k // 2, nc), k // (2 * nc), lax.rem(k, 2)
        one, two = roots_r[c, ch, p, 0], roots_r[c, ch, p, 1]
        first[k], second[k] = one + two, -one * two
        gain[k] = (1.0 - one) * (1.0 - two)

    def advance(k, states):
        out = []
        for b in range(ny):
            at = b * block + k
            f, s = first[at], second[at]
            out.append(tuple((f * y1 + s * y2, y1) for y1, y2 in states[b]))
        return tuple(out)

    begin = []
    for b in range(ny):
        f0, s0, f1, s1 = first[b * block], second[b * block], first[b * block + 1], second[b * block + 1]
        begin.append(((f1 * f0 + s1, f0), (f1 * s0, s0)))
    done = lax.fori_loop(2, block, advance, tuple(begin))
    for b in range(ny):
        (a, c), (d, e) = done[b]
        for n, value in enumerate((a, d, c, e)):
            trans[half, 4 * b + n] = value
    trans_copy = remote(
        trans.at[half, chip], trans.at[half, chip], trans_sem.at[0], trans_sem.at[1], partner
    )

    @pl.when(jnp.logical_not(leads))
    def _():
        trans_copy.start()

    @pl.when(has_up)
    def _():
        down.wait_recv()

    @pl.when(jnp.logical_not(has_up))
    def _():
        above[...] = jnp.zeros_like(above)

    @pl.when(has_down)
    def _():
        up.wait_recv()

    @pl.when(jnp.logical_not(has_down))
    def _():
        below[...] = jnp.zeros_like(below)

    for p in range(2):
        over = jnp.concatenate([above[p], x_ref[p, 0:64]], 0)
        to_flat(2, p, dot3(top, pieces(over)))
    for n in outer_chunks[:1]:
        if len(outer_chunks) == 2:
            spread_rows(n)
    for p in range(2):
        under = jnp.concatenate([x_ref[p, 64:128], below[p]], 0)
        to_flat(3, p, dot3(bottom, pieces(under)))
    spread_rows(outer_chunks[-1])

    def back_scan(slot, begin, keep):
        def step(i, states):
            out = []
            for b, (u, t) in enumerate(states):
                at = b * block + block - 1 - i
                z = recv[slot, at] + u
                if keep:
                    recv[slot, at] = gain[at] * z
                out.append((first[at] * z + t, second[at] * z))
            return tuple(out)

        return lax.fori_loop(2, block, step, step(1, step(0, begin)))

    def fore_scan(slot, begin, keep):
        def step(k, states):
            out = []
            for b, (y1, y2) in enumerate(states):
                at = b * block + k
                y = gain[at] * recv[slot, at] + first[at] * y1 + second[at] * y2
                if keep:
                    recv[slot, at] = y
                out.append((y, y1))
            return tuple(out)

        return lax.fori_loop(2, block, step, step(1, step(0, begin)))

    zero = jnp.zeros((EIGHTHS, 128), F32)
    nothing = [(zero, zero)] * ny

    def slots(n):
        return range(CHUNKS[n][0], sum(CHUNKS[n]))

    def hand_over(buf, sems, n, scan, first_send=False):
        for slot in slots(n):
            for b, (s1, s2) in enumerate(scan(slot, nothing, False)):
                buf[slot, half, b, 0] = s1
                buf[slot, half, b, 1] = s2
        if first_send:

            @pl.when(leads)
            def _():
                pl.semaphore_wait(ready_sem, 1)
                trans_copy.start()

        at = pl.ds(*CHUNKS[n])
        remote(
            buf.at[at, half], buf.at[at, half], sems.at[0, n], sems.at[1, n], partner
        ).start()

    def x_twice(slot):
        n = 2 * group * EIGHTHS
        eighth = lax.rem(lax.broadcasted_iota(jnp.int32, (n, 128), 0), EIGHTHS)
        lane = lax.broadcasted_iota(jnp.int32, (n, 128), 1)
        own = recv[slot].reshape(n, 128)
        matrix = (kx_high[...], kx_low[...])
        for _ in range(2):
            before = jnp.where(eighth == 0, 0.0, pltpu.roll(own, 1, 0))
            after = jnp.where(eighth == EIGHTHS - 1, 0.0, pltpu.roll(own, n - 1, 0))
            sides = jnp.where(lane < 64, after, before)
            own = dot3(pieces(jnp.concatenate([own, sides], 1)), matrix)
        recv[slot] = own.reshape(2 * group, EIGHTHS, 128)

    def far_state(buf, n):
        arrived(buf.at[pl.ds(*CHUNKS[n]), 1 - half], (end_sem if buf is ends else end2_sem).at[1, n])

    for n in range(len(CHUNKS)):
        arrived(recv.at[pl.ds(*CHUNKS[n]), pl.ds(0, 2 * group - 2)], in_sem.at[n])
        hand_over(ends, end_sem, n, back_scan, n == 0)
        if n == 1:
            trans_copy.wait_recv()
            for gz, _ in peers(True):
                remote(
                    trans.at[1 - half, chip], trans.at[1 - half, chip],
                    trans_sem.at[2], trans_sem.at[3], gz,
                ).start()

    arrived(trans.at[1 - half, pl.ds(0, chips - 1)], trans_sem.at[3])

    for n in range(len(CHUNKS)):
        far_state(ends, n)
        for slot in slots(n):
            u, t = zero, zero
            for j in reversed(range(ny * nz)):
                b, z = j // nz, j % nz
                starts[slot, z, b, 0], starts[slot, z, b, 1] = u, t
                a11, a12, a21, a22 = (trans[z, 4 * b + i] for i in range(4))
                u, t = a11 * u + a21 * t + ends[slot, z, b, 0], a12 * u + a22 * t + ends[slot, z, b, 1]
            begin = [(starts[slot, half, b, 0], starts[slot, half, b, 1]) for b in range(ny)]
            back_scan(slot, begin, True)
            x_twice(slot)
        hand_over(ends2, end2_sem, n, fore_scan)

    for n in range(len(CHUNKS)):
        far_state(ends2, n)
        for slot in slots(n):
            y1, y2 = zero, zero
            for j in range(ny * nz):
                b, z = j // nz, j % nz
                starts[slot, z, b, 0], starts[slot, z, b, 1] = y1, y2
                a11, a12, a21, a22 = (trans[z, 4 * b + i] for i in range(4))
                y1, y2 = (
                    a11 * y1 + a12 * y2 + ends2[slot, z, b, 0],
                    a21 * y1 + a22 * y2 + ends2[slot, z, b, 1],
                )
            begin = [(starts[slot, half, b, 0], starts[slot, half, b, 1]) for b in range(ny)]
            fore_scan(slot, begin, True)
        at = pl.ds(*CHUNKS[n])
        for gz, place in peers():
            remote(
                recv.at[at, pl.ds(2 * place, 2)], back.at[at, :, flat(me)],
                home_s.at[n], home_r.at[n], gz,
            ).start()
        back[at, :, flat(me)] = recv[at, pl.ds(2 * me, 2)]

    for n in range(len(CHUNKS)):
        arrived(back.at[pl.ds(*CHUNKS[n]), :, pl.ds(0, (group - 1) * EIGHTHS)], home_r.at[n])
        for slot in slots(n):
            to = RUNS[slot]
            for p in range(2):
                for e in range(EIGHTHS):
                    o_ref[p, to : to + 32, 128 * e : 128 * e + 128] = back[
                        slot, p, pl.ds(e, 32, stride=EIGHTHS), :
                    ]

    @pl.when(has_up)
    def _():
        up.wait_send()

    @pl.when(has_down)
    def _():
        down.wait_send()

    trans_copy.wait_send()
    root_copy.wait_send()
    arrived(trans.at[1 - half, pl.ds(0, chips - 1)], trans_sem.at[2])
    arrived(roots_r.at[0, pl.ds(0, chips - 1)], root_sem.at[0])
    for n in range(len(CHUNKS)):
        at = pl.ds(*CHUNKS[n])
        arrived(send.at[at, :, pl.ds(0, (group - 1) * EIGHTHS)], out_sem.at[n])
        arrived(ends.at[at, 0], end_sem.at[0, n])
        arrived(ends2.at[at, 0], end2_sem.at[0, n])
        arrived(back.at[at, :, pl.ds(0, (group - 1) * EIGHTHS)], home_s.at[n])


def build(sizes, n_slabs):
    ny, nz, nxx, nc = sizes
    chips = ny * nxx
    group = chips * nc
    steps = len(CHUNKS)

    def body(probe_fields, root_one, root_two, lateral_kernel_taps, dilations):
        dma, vmem, smem = pltpu.SemaphoreType.DMA, pltpu.VMEM, pltpu.SMEM
        out = pl.pallas_call(
            functools.partial(kernel, sizes, n_slabs),
            out_shape=jax.ShapeDtypeStruct((2, 128, 1024), F32),
            in_specs=[pl.BlockSpec(memory_space=pltpu.HBM)] * 5,
            out_specs=pl.BlockSpec(memory_space=vmem),
            scratch_shapes=[
                vmem((2, 128, 1024), F32),
                vmem((2, 1024), F32),
                vmem((2, 1024), F32),
                smem((2, 3), F32),
                smem((2,), jnp.int32),
                vmem((4, 2, 256, 128), F32),
                vmem((4, 2 * group, 8, 128), F32),
                vmem((4, 2, 256, 128), F32),
                vmem((2, 2, 8, 128), F32),
                vmem((nc, chips, 2, 2, 8, 128), F32),
                vmem((2 * group, 8, 128), F32),
                vmem((2 * group, 8, 128), F32),
                vmem((2 * group, 8, 128), F32),
                vmem((2, 32, 1024), F32),
                vmem((2, 32, 1024), F32),
                vmem((256, 128), BF16),
                vmem((256, 128), BF16),
                vmem((nz, 4 * ny, 8, 128), F32),
                vmem((4, nz, ny, 2, 8, 128), F32),
                vmem((4, nz, ny, 2, 8, 128), F32),
                vmem((4, nz, ny, 2, 8, 128), F32),
                dma((5,)),
                pltpu.SemaphoreType.REGULAR,
                dma((4,)),
                dma((4,)),
                dma((steps,)),
                dma((steps,)),
                dma((4,)),
                dma((2, steps)),
                dma((2, steps)),
                dma((steps,)),
                dma((steps,)),
            ],
            compiler_params=pltpu.CompilerParams(
                collective_id=0, has_side_effects=True, vmem_limit_bytes=67043328
            ),
        )(probe_fields[0], root_one, root_two, lateral_kernel_taps, dilations)
        return out[None]

    return body


def solution(mesh):
    placed = (P(None, "gz", "gy", None), P("gz", None), P("gz", None), P(), P())
    return jax.shard_map(
        build(SIZES, mesh.shape["gy"]),
        mesh=mesh,
        in_specs=placed,
        out_specs=P(None, "gz", "gy", None),
        check_vma=False,
    )
```

```python
import functools
import jax
import jax.numpy as jnp
from jax import lax
from jax.experimental import pallas as pl
from jax.experimental.pallas import tpu as pltpu
from jax.sharding import PartitionSpec as P

MESH = pl.DeviceIdType.MESH
F32 = jnp.float32
BF16 = jnp.bfloat16
SIZES = (4, 2, 4, 2)
MARGIN = 16
EIGHTHS = 8
RUNS = (32, 64, 0, 96)
CHUNKS = ((0, 1), (1, 1), (2, 1), (3, 1))


def pieces(a):
    high = a.astype(BF16)
    return high, (a - high.astype(F32)).astype(BF16)


def dot3(a, b):
    (ah, al), (bh, bl) = a, b
    dot = functools.partial(jnp.dot, preferred_element_type=F32)
    return dot(ah, bh) + (dot(ah, bl) + dot(al, bh))


def stencil(away, taps, row, step):
    centre, near, far = taps[row, 0], taps[row, 1], taps[row, 2]
    weight = jnp.where(away == 0, centre, 0.0)
    weight = jnp.where(away == step, near, weight)
    weight = jnp.where(away == 2 * step, far, weight)
    return weight / (centre + 2.0 * (near + far))


def kernel(
    sizes, n_slabs, x_hbm, one_hbm, two_hbm, taps_hbm, dils_hbm, o_ref,
    x_ref, one_ref, two_ref, taps, dils, send, recv, back, roots_s, roots_r, first, second, gain,
    above, below, kx_high, kx_low, entry, trans, ends, ends2, starts,
    load_sem, ready_sem, row_sem, root_sem, share_sem, halo_sem, out_sem, in_sem, trans_sem, end_sem, end2_sem, home_s, home_r,
):
    ny, nz, nxx, nc = sizes
    chips = ny * nxx
    group = chips * nc
    block = nxx * nc * 2
    g, gy = lax.axis_index("gz"), lax.axis_index("gy")
    core, col = lax.rem(g, nc), lax.rem(g // nc, nxx)
    half, line = lax.rem(g // (nc * nxx), nz), g // (nc * nxx * nz)
    chip = line * nxx + col
    me = chip * nc + core

    def gz_of(yy, zz, xx, cc):
        return ((yy * nz + zz) * nxx + xx) * nc + cc

    partner, sibling = gz_of(line, 1 - half, col, core), gz_of(line, half, col, 1 - core)

    def reach(n, step):
        return min(step, n - step)

    steps = [(a, b, c) for a in range(ny) for b in range(nxx) for c in range(nc)][1:]
    steps.sort(key=lambda s: (-reach(ny, s[0]) - reach(nxx, s[1]), -min(s[0], 1) - min(s[1], 1)))

    def peers(kind="all"):
        for a, b, c in steps:
            if not {"all": True, "row": a == 0, "core": a and not c, "alike": not c}[kind]:
                continue
            yy, xx, cc = lax.rem(line + a, ny), lax.rem(col + b, nxx), lax.rem(core + c, nc)
            yield gz_of(yy, half, xx, cc), (yy * nxx + xx) * nc + cc

    def remote(src, dst, s, r, gz, slab=gy):
        return pltpu.make_async_remote_copy(
            src, dst, s, r, device_id=(gz, slab), device_id_type=MESH
        )

    def arrived(ref, sem):
        pltpu.make_async_copy(ref, ref, sem).wait()

    def flat(place):
        return pl.ds(pl.multiple_of(place * EIGHTHS, EIGHTHS), EIGHTHS)

    loads = [
        pltpu.make_async_copy(a, b, load_sem.at[i])
        for i, (a, b) in enumerate(
            (
                (one_hbm, one_ref),
                (two_hbm, two_ref),
                (taps_hbm, taps),
                (dils_hbm, dils),
                (x_hbm, x_ref),
            )
        )
    ]
    for copy in loads:
        copy.start()

    has_up, has_down = gy > 0, gy < n_slabs - 1

    barrier = pltpu.get_barrier_semaphore()

    def hello(gz, slab):
        pl.semaphore_signal(barrier, inc=1, device_id=(gz, slab), device_id_type=MESH)

    leads = half == 0

    @pl.when(leads)
    def _():
        hello(partner, gy)

    @pl.when(has_up)
    def _():
        hello(g, gy - 1)

    @pl.when(has_down)
    def _():
        hello(g, gy + 1)

    for gz, _ in peers():
        hello(gz, gy)

    loads[0].wait()
    loads[1].wait()
    for p in range(2):
        for e in range(EIGHTHS):
            lanes = slice(128 * e, 128 * e + 128)
            roots_s[p, 0, e : e + 1, :] = one_ref[p : p + 1, lanes]
            roots_s[p, 1, e : e + 1, :] = two_ref[p : p + 1, lanes]

    loads[2].wait()
    loads[3].wait()
    exact = functools.partial(jnp.dot, precision=lax.Precision.HIGHEST, preferred_element_type=F32)

    def ky(n_out, n_in):
        i = lax.broadcasted_iota(jnp.int32, (n_out, n_in), 0)
        j = lax.broadcasted_iota(jnp.int32, (n_out, n_in), 1)
        return stencil(jnp.abs(i - j + MARGIN), taps, 1, dils[1])

    def to_flat(slot, p, value):
        for e in range(EIGHTHS):
            send[slot, p, pl.ds(e, 32, stride=EIGHTHS), :] = value[:, 128 * e : 128 * e + 128]

    inner = pieces(exact(ky(64, 96), ky(96, 128)))
    loads[4].wait()
    for p in range(2):
        middle = dot3(inner, pieces(x_ref[p]))
        to_flat(0, p, middle[:32])
        to_flat(1, p, middle[32:])

    pl.semaphore_wait(
        barrier, group - 1 + half + has_up.astype(jnp.int32) + has_down.astype(jnp.int32)
    )

    @pl.when(jnp.logical_not(leads))
    def _():
        pl.semaphore_signal(ready_sem, inc=1, device_id=(partner, gy), device_id_type=MESH)

    for gz, _ in peers("row"):
        remote(roots_s, roots_r.at[core, chip], row_sem.at[0], row_sem.at[1], gz).start()
    for gz, _ in peers("core"):
        remote(roots_s, roots_r.at[core, chip], root_sem.at[0], root_sem.at[1], gz).start()
    roots_r[core, chip] = roots_s[...]
    up = remote(x_ref.at[:, 0:32], below, halo_sem.at[0], halo_sem.at[2], g, gy - 1)
    down = remote(x_ref.at[:, 96:128], above, halo_sem.at[1], halo_sem.at[3], g, gy + 1)

    @pl.when(has_up)
    def _():
        up.start()

    @pl.when(has_down)
    def _():
        down.start()

    def spread_rows(n):
        at = pl.ds(*CHUNKS[n])
        for gz, place in peers():
            remote(
                send.at[at, :, flat(place)], recv.at[at, pl.ds(2 * me, 2)],
                out_sem.at[n], in_sem.at[n], gz,
            ).start()
        recv[at, pl.ds(2 * me, 2)] = send[at, :, flat(me)]

    inner_chunks = [n for n, (s, _) in enumerate(CHUNKS) if s < 2]
    outer_chunks = [n for n, (s, _) in enumerate(CHUNKS) if s >= 2]
    spread_rows(inner_chunks[0])

    i = lax.broadcasted_iota(jnp.int32, (256, 128), 0)
    j = lax.broadcasted_iota(jnp.int32, (256, 128), 1)
    kx = stencil(jnp.abs(jnp.where(i < 192, i, i - 256) - j), taps, 0, dils[0])
    kx_high[...], kx_low[...] = pieces(kx)

    head, tail = ky(32, 64), ky(64, 96)
    mid = lax.broadcasted_iota(jnp.int32, (64, 96), 0)
    top = pieces(exact(head, jnp.where(has_up | (mid >= MARGIN), tail, 0.0)))
    bottom = pieces(exact(head, jnp.where(has_down | (mid < 64 - MARGIN), tail, 0.0)))

    def transition(roots_of):
        (f0, s0), (f, s) = (
            (one + two, -one * two) for one, two in (roots_of(0), roots_of(1))
        )
        y = [(f * f0 + s, f0), (f * s0, s0)]
        for k in range(2, block):
            one, two = roots_of(k)
            f, s = one + two, -one * two
            y = [(f * y1 + s * y2, y1) for y1, y2 in y]
        (a, c), (d, e) = y
        return a, d, c, e

    def roots_at(row):
        def of(k):
            c, ch, p = k // 2 % nc, row * nxx + k // (2 * nc), k % 2
            return roots_r[c, ch, p, 0], roots_r[c, ch, p, 1]

        return of

    arrived(roots_r.at[0, pl.ds(0, nxx * nc - 1)], row_sem.at[1])
    for n, value in enumerate(transition(roots_at(line))):
        entry[n] = value
    trans_copy = remote(
        entry.at[col], trans.at[half, chip], trans_sem.at[0], trans_sem.at[1], partner
    )

    @pl.when(jnp.logical_not(leads))
    def _():
        trans_copy.start()

    arrived(roots_r.at[0, pl.ds(0, chips - nxx)], root_sem.at[1])
    root_copies = []
    for n in range(1, ny):
        other = roots_r.at[core, pl.ds(lax.rem(line + n, ny) * nxx, nxx)]
        root_copies.append(remote(other, other, share_sem.at[0, n - 1], share_sem.at[1, n - 1], sibling))
    for copy in root_copies:
        copy.start()
    for n in inner_chunks[1:]:
        spread_rows(n)

    @pl.when(has_up)
    def _():
        down.wait_recv()

    @pl.when(jnp.logical_not(has_up))
    def _():
        above[...] = jnp.zeros_like(above)

    @pl.when(has_down)
    def _():
        up.wait_recv()

    @pl.when(jnp.logical_not(has_down))
    def _():
        below[...] = jnp.zeros_like(below)

    for p in range(2):
        over = jnp.concatenate([above[p], x_ref[p, 0:64]], 0)
        to_flat(2, p, dot3(top, pieces(over)))
    if len(outer_chunks) == 2:
        spread_rows(outer_chunks[0])
    for p in range(2):
        under = jnp.concatenate([x_ref[p, 64:128], below[p]], 0)
        to_flat(3, p, dot3(bottom, pieces(under)))
    spread_rows(outer_chunks[-1])

    for copy in root_copies:
        copy.wait_recv()

    for ch in range(chips):
        for c in range(nc):
            one, two = roots_r[c, ch, :, 0], roots_r[c, ch, :, 1]
            at = pl.ds(2 * (nc * ch + c), 2)
            first[at], second[at] = one + two, -one * two
            gain[at] = (1.0 - one) * (1.0 - two)
    for b in range(ny):
        for n, value in enumerate(transition(roots_at(b))):
            trans[half, 4 * b + n] = value

    def back_scan(slot, begin, keep):
        def step(i, states):
            out = []
            for b, (u, t) in enumerate(states):
                at = b * block + block - 1 - i
                z = recv[slot, at] + u
                if keep:
                    recv[slot, at] = gain[at] * z
                out.append((first[at] * z + t, second[at] * z))
            return tuple(out)

        return lax.fori_loop(2, block, step, step(1, step(0, begin)))

    def fore_scan(slot, begin, keep):
        def step(k, states):
            out = []
            for b, (y1, y2) in enumerate(states):
                at = b * block + k
                y = gain[at] * recv[slot, at] + first[at] * y1 + second[at] * y2
                if keep:
                    recv[slot, at] = y
                out.append((y, y1))
            return tuple(out)

        return lax.fori_loop(2, block, step, step(1, step(0, begin)))

    zero = jnp.zeros((EIGHTHS, 128), F32)
    nothing = [(zero, zero)] * ny

    def slots(n):
        return range(CHUNKS[n][0], sum(CHUNKS[n]))

    def hand_over(buf, sems, n, scan, first_send=False):
        for slot in slots(n):
            for b, (s1, s2) in enumerate(scan(slot, nothing, False)):
                buf[slot, half, b, 0] = s1
                buf[slot, half, b, 1] = s2
        if first_send:

            @pl.when(leads)
            def _():
                pl.semaphore_wait(ready_sem, 1)
                trans_copy.start()

        at = pl.ds(*CHUNKS[n])
        remote(
            buf.at[at, half], buf.at[at, half], sems.at[0, n], sems.at[1, n], partner
        ).start()

    def x_twice(slot):
        n = 2 * group * EIGHTHS
        eighth = lax.rem(lax.broadcasted_iota(jnp.int32, (n, 128), 0), EIGHTHS)
        lane = lax.broadcasted_iota(jnp.int32, (n, 128), 1)
        own = recv[slot].reshape(n, 128)
        matrix = (kx_high[...], kx_low[...])
        for _ in range(2):
            before = jnp.where(eighth == 0, 0.0, pltpu.roll(own, 1, 0))
            after = jnp.where(eighth == EIGHTHS - 1, 0.0, pltpu.roll(own, n - 1, 0))
            sides = jnp.where(lane < 64, after, before)
            own = dot3(pieces(jnp.concatenate([own, sides], 1)), matrix)
        recv[slot] = own.reshape(2 * group, EIGHTHS, 128)

    def far_state(buf, n):
        arrived(buf.at[pl.ds(*CHUNKS[n]), 1 - half], (end_sem if buf is ends else end2_sem).at[1, n])

    for n in range(len(CHUNKS)):
        arrived(recv.at[pl.ds(*CHUNKS[n]), pl.ds(0, 2 * group - 2)], in_sem.at[n])
        hand_over(ends, end_sem, n, back_scan, n == 0)
        if n == 1:
            trans_copy.wait_recv()
            for gz, _ in peers("alike"):
                remote(
                    trans.at[1 - half, chip], trans.at[1 - half, chip],
                    trans_sem.at[2], trans_sem.at[3], gz,
                ).start()

    arrived(trans.at[1 - half, pl.ds(0, chips - 1)], trans_sem.at[3])

    for n in range(len(CHUNKS)):
        far_state(ends, n)
        for slot in slots(n):
            u, t = zero, zero
            for j in reversed(range(ny * nz)):
                b, z = j // nz, j % nz
                starts[slot, z, b, 0], starts[slot, z, b, 1] = u, t
                a11, a12, a21, a22 = (trans[z, 4 * b + i] for i in range(4))
                u, t = a11 * u + a21 * t + ends[slot, z, b, 0], a12 * u + a22 * t + ends[slot, z, b, 1]
            begin = [(starts[slot, half, b, 0], starts[slot, half, b, 1]) for b in range(ny)]
            back_scan(slot, begin, True)
            x_twice(slot)
        hand_over(ends2, end2_sem, n, fore_scan)

    for n in range(len(CHUNKS)):
        far_state(ends2, n)
        for slot in slots(n):
            y1, y2 = zero, zero
            for j in range(ny * nz):
                b, z = j // nz, j % nz
                starts[slot, z, b, 0], starts[slot, z, b, 1] = y1, y2
                a11, a12, a21, a22 = (trans[z, 4 * b + i] for i in range(4))
                y1, y2 = (
                    a11 * y1 + a12 * y2 + ends2[slot, z, b, 0],
                    a21 * y1 + a22 * y2 + ends2[slot, z, b, 1],
                )
            begin = [(starts[slot, half, b, 0], starts[slot, half, b, 1]) for b in range(ny)]
            fore_scan(slot, begin, True)
        at = pl.ds(*CHUNKS[n])
        for gz, place in peers():
            remote(
                recv.at[at, pl.ds(2 * place, 2)], back.at[at, :, flat(me)],
                home_s.at[n], home_r.at[n], gz,
            ).start()
        back[at, :, flat(me)] = recv[at, pl.ds(2 * me, 2)]

    for n in range(len(CHUNKS)):
        arrived(back.at[pl.ds(*CHUNKS[n]), :, pl.ds(0, (group - 1) * EIGHTHS)], home_r.at[n])
        for slot in slots(n):
            to = RUNS[slot]
            for p in range(2):
                for e in range(EIGHTHS):
                    o_ref[p, to : to + 32, 128 * e : 128 * e + 128] = back[
                        slot, p, pl.ds(e, 32, stride=EIGHTHS), :
                    ]

    @pl.when(has_up)
    def _():
        up.wait_send()

    @pl.when(has_down)
    def _():
        down.wait_send()

    trans_copy.wait_send()
    for copy in root_copies:
        copy.wait_send()
    arrived(trans.at[1 - half, pl.ds(0, chips - 1)], trans_sem.at[2])
    arrived(roots_r.at[0, pl.ds(0, nxx * nc - 1)], row_sem.at[0])
    arrived(roots_r.at[0, pl.ds(0, chips - nxx)], root_sem.at[0])
    for n in range(len(CHUNKS)):
        at = pl.ds(*CHUNKS[n])
        arrived(send.at[at, :, pl.ds(0, (group - 1) * EIGHTHS)], out_sem.at[n])
        arrived(ends.at[at, 0], end_sem.at[0, n])
        arrived(ends2.at[at, 0], end2_sem.at[0, n])
        arrived(back.at[at, :, pl.ds(0, (group - 1) * EIGHTHS)], home_s.at[n])


def build(sizes, n_slabs):
    ny, nz, nxx, nc = sizes
    chips = ny * nxx
    group = chips * nc
    steps = len(CHUNKS)

    def body(probe_fields, root_one, root_two, lateral_kernel_taps, dilations):
        dma, vmem, smem = pltpu.SemaphoreType.DMA, pltpu.VMEM, pltpu.SMEM
        out = pl.pallas_call(
            functools.partial(kernel, sizes, n_slabs),
            out_shape=jax.ShapeDtypeStruct((2, 128, 1024), F32),
            in_specs=[pl.BlockSpec(memory_space=pltpu.HBM)] * 5,
            out_specs=pl.BlockSpec(memory_space=vmem),
            scratch_shapes=[
                vmem((2, 128, 1024), F32),
                vmem((2, 1024), F32),
                vmem((2, 1024), F32),
                smem((2, 3), F32),
                smem((2,), jnp.int32),
                vmem((4, 2, 256, 128), F32),
                vmem((4, 2 * group, 8, 128), F32),
                vmem((4, 2, 256, 128), F32),
                vmem((2, 2, 8, 128), F32),
                vmem((nc, chips, 2, 2, 8, 128), F32),
                vmem((2 * group, 8, 128), F32),
                vmem((2 * group, 8, 128), F32),
                vmem((2 * group, 8, 128), F32),
                vmem((2, 32, 1024), F32),
                vmem((2, 32, 1024), F32),
                vmem((256, 128), BF16),
                vmem((256, 128), BF16),
                vmem((4, 8, 128), F32),
                vmem((nz, 4 * ny, 8, 128), F32),
                vmem((4, nz, ny, 2, 8, 128), F32),
                vmem((4, nz, ny, 2, 8, 128), F32),
                vmem((4, nz, ny, 2, 8, 128), F32),
                dma((5,)),
                pltpu.SemaphoreType.REGULAR,
                dma((2,)),
                dma((2,)),
                dma((2, ny - 1)),
                dma((4,)),
                dma((steps,)),
                dma((steps,)),
                dma((4,)),
                dma((2, steps)),
                dma((2, steps)),
                dma((steps,)),
                dma((steps,)),
            ],
            compiler_params=pltpu.CompilerParams(
                collective_id=0, has_side_effects=True, vmem_limit_bytes=48 << 20
            ),
        )(
            *(
                pltpu.with_memory_space_constraint(a, pltpu.HBM)
                for a in (probe_fields[0], root_one, root_two, lateral_kernel_taps, dilations)
            )
        )
        return out[None]

    return body


def solution(mesh):
    placed = (P(None, "gz", "gy", None), P("gz", None), P("gz", None), P(), P())
    return jax.shard_map(
        build(SIZES, mesh.shape["gy"]),
        mesh=mesh,
        in_specs=placed,
        out_specs=P(None, "gz", "gy", None),
        check_vma=False,
    )
```

```python
import functools
import jax
import jax.numpy as jnp
from jax import lax
from jax.experimental import pallas as pl
from jax.experimental.pallas import tpu as pltpu
from jax.sharding import PartitionSpec as P

MESH = pl.DeviceIdType.MESH
F32 = jnp.float32
BF16 = jnp.bfloat16
SIZES = (4, 2, 4, 2)
MARGIN = 16
EIGHTHS = 8
RUNS = (32, 64, 0, 96)
CHUNKS = ((0, 1), (1, 1), (2, 1), (3, 1))


def pieces(a):
    high = a.astype(BF16)
    return high, (a - high.astype(F32)).astype(BF16)


def dot3(a, b):
    (ah, al), (bh, bl) = a, b
    dot = functools.partial(jnp.dot, preferred_element_type=F32)
    return dot(ah, bh) + (dot(ah, bl) + dot(al, bh))


def stencil(away, taps, row, step):
    centre, near, far = taps[row, 0], taps[row, 1], taps[row, 2]
    weight = jnp.where(away == 0, centre, 0.0)
    weight = jnp.where(away == step, near, weight)
    weight = jnp.where(away == 2 * step, far, weight)
    return weight / (centre + 2.0 * (near + far))


def kernel(
    sizes, n_slabs, x_hbm, one_hbm, two_hbm, taps_hbm, dils_hbm, o_ref,
    x_ref, one_ref, two_ref, taps, dils, send, recv, back, roots_s, roots_r, first, second, gain,
    above, below, kx_high, kx_low, entry, trans, ends, ends2,
    load_sem, ready_sem, row_sem, root_sem, share_sem, halo_sem, out_sem, in_sem, trans_sem, end_sem, end2_sem, home_s, home_r,
):
    ny, nz, nxx, nc = sizes
    chips = ny * nxx
    group = chips * nc
    block = nxx * nc * 2
    g, gy = lax.axis_index("gz"), lax.axis_index("gy")
    core, col = lax.rem(g, nc), lax.rem(g // nc, nxx)
    half, line = lax.rem(g // (nc * nxx), nz), g // (nc * nxx * nz)
    chip = line * nxx + col
    me = chip * nc + core

    def gz_of(yy, zz, xx, cc):
        return ((yy * nz + zz) * nxx + xx) * nc + cc

    partner, sibling = gz_of(line, 1 - half, col, core), gz_of(line, half, col, 1 - core)

    def reach(n, step):
        return min(step, n - step)

    steps = [(a, b, c) for a in range(ny) for b in range(nxx) for c in range(nc)][1:]
    steps.sort(key=lambda s: (-reach(ny, s[0]) - reach(nxx, s[1]), -min(s[0], 1) - min(s[1], 1)))

    def peers(kind="all"):
        for a, b, c in steps:
            if not {"all": True, "row": a == 0, "core": a and not c, "alike": not c}[kind]:
                continue
            yy, xx, cc = lax.rem(line + a, ny), lax.rem(col + b, nxx), lax.rem(core + c, nc)
            yield gz_of(yy, half, xx, cc), (yy * nxx + xx) * nc + cc

    def remote(src, dst, s, r, gz, slab=gy):
        return pltpu.make_async_remote_copy(
            src, dst, s, r, device_id=(gz, slab), device_id_type=MESH
        )

    def arrived(ref, sem):
        pltpu.make_async_copy(ref, ref, sem).wait()

    def flat(place):
        return pl.ds(pl.multiple_of(place * EIGHTHS, EIGHTHS), EIGHTHS)

    loads = [
        pltpu.make_async_copy(a, b, load_sem.at[i])
        for i, (a, b) in enumerate(
            (
                (one_hbm, one_ref),
                (two_hbm, two_ref),
                (taps_hbm, taps),
                (dils_hbm, dils),
                (x_hbm, x_ref),
            )
        )
    ]
    for copy in loads:
        copy.start()

    has_up, has_down = gy > 0, gy < n_slabs - 1

    barrier = pltpu.get_barrier_semaphore()

    def hello(gz, slab):
        pl.semaphore_signal(barrier, inc=1, device_id=(gz, slab), device_id_type=MESH)

    leads = half == 0

    @pl.when(leads)
    def _():
        hello(partner, gy)

    @pl.when(has_up)
    def _():
        hello(g, gy - 1)

    @pl.when(has_down)
    def _():
        hello(g, gy + 1)

    for gz, _ in peers():
        hello(gz, gy)

    loads[0].wait()
    loads[1].wait()
    for p in range(2):
        for e in range(EIGHTHS):
            lanes = slice(128 * e, 128 * e + 128)
            roots_s[p, 0, e : e + 1, :] = one_ref[p : p + 1, lanes]
            roots_s[p, 1, e : e + 1, :] = two_ref[p : p + 1, lanes]

    loads[2].wait()
    loads[3].wait()
    exact = functools.partial(jnp.dot, precision=lax.Precision.HIGHEST, preferred_element_type=F32)

    def ky(n_out, n_in):
        i = lax.broadcasted_iota(jnp.int32, (n_out, n_in), 0)
        j = lax.broadcasted_iota(jnp.int32, (n_out, n_in), 1)
        return stencil(jnp.abs(i - j + MARGIN), taps, 1, dils[1])

    def to_flat(slot, p, value):
        for e in range(EIGHTHS):
            send[slot, p, pl.ds(e, 32, stride=EIGHTHS), :] = value[:, 128 * e : 128 * e + 128]

    inner = pieces(exact(ky(64, 96), ky(96, 128)))
    loads[4].wait()
    for p in range(2):
        middle = dot3(inner, pieces(x_ref[p]))
        to_flat(0, p, middle[:32])
        to_flat(1, p, middle[32:])

    pl.semaphore_wait(
        barrier, group - 1 + half + has_up.astype(jnp.int32) + has_down.astype(jnp.int32)
    )

    @pl.when(jnp.logical_not(leads))
    def _():
        pl.semaphore_signal(ready_sem, inc=1, device_id=(partner, gy), device_id_type=MESH)

    for gz, _ in peers("row"):
        remote(roots_s, roots_r.at[core, chip], row_sem.at[0], row_sem.at[1], gz).start()
    for gz, _ in peers("core"):
        remote(roots_s, roots_r.at[core, chip], root_sem.at[0], root_sem.at[1], gz).start()
    roots_r[core, chip] = roots_s[...]
    up = remote(x_ref.at[:, 0:32], below, halo_sem.at[0], halo_sem.at[2], g, gy - 1)
    down = remote(x_ref.at[:, 96:128], above, halo_sem.at[1], halo_sem.at[3], g, gy + 1)

    @pl.when(has_up)
    def _():
        up.start()

    @pl.when(has_down)
    def _():
        down.start()

    def spread_rows(n):
        at = pl.ds(*CHUNKS[n])
        for gz, place in peers():
            remote(
                send.at[at, :, flat(place)], recv.at[at, pl.ds(2 * me, 2)],
                out_sem.at[n], in_sem.at[n], gz,
            ).start()
        recv[at, pl.ds(2 * me, 2)] = send[at, :, flat(me)]

    inner_chunks = [n for n, (s, _) in enumerate(CHUNKS) if s < 2]
    outer_chunks = [n for n, (s, _) in enumerate(CHUNKS) if s >= 2]
    spread_rows(inner_chunks[0])

    i = lax.broadcasted_iota(jnp.int32, (256, 128), 0)
    j = lax.broadcasted_iota(jnp.int32, (256, 128), 1)
    kx = stencil(jnp.abs(jnp.where(i < 192, i, i - 256) - j), taps, 0, dils[0])
    kx_high[...], kx_low[...] = pieces(kx)

    head, tail = ky(32, 64), ky(64, 96)
    mid = lax.broadcasted_iota(jnp.int32, (64, 96), 0)
    top = pieces(exact(head, jnp.where(has_up | (mid >= MARGIN), tail, 0.0)))
    bottom = pieces(exact(head, jnp.where(has_down | (mid < 64 - MARGIN), tail, 0.0)))

    def transition(roots_of):
        (f0, s0), (f, s) = (
            (one + two, -one * two) for one, two in (roots_of(0), roots_of(1))
        )
        y = [(f * f0 + s, f0), (f * s0, s0)]
        for k in range(2, block):
            one, two = roots_of(k)
            f, s = one + two, -one * two
            y = [(f * y1 + s * y2, y1) for y1, y2 in y]
        (a, c), (d, e) = y
        return a, d, c, e

    def roots_at(row):
        def of(k):
            c, ch, p = k // 2 % nc, row * nxx + k // (2 * nc), k % 2
            return roots_r[c, ch, p, 0], roots_r[c, ch, p, 1]

        return of

    arrived(roots_r.at[0, pl.ds(0, nxx * nc - 1)], row_sem.at[1])
    for n, value in enumerate(transition(roots_at(line))):
        entry[n] = value
    trans_copy = remote(
        entry.at[col], trans.at[half, chip], trans_sem.at[0], trans_sem.at[1], partner
    )

    @pl.when(jnp.logical_not(leads))
    def _():
        trans_copy.start()

    arrived(roots_r.at[0, pl.ds(0, chips - nxx)], root_sem.at[1])
    root_copies = []
    for n in range(1, ny):
        other = roots_r.at[core, pl.ds(lax.rem(line + n, ny) * nxx, nxx)]
        root_copies.append(remote(other, other, share_sem.at[0, n - 1], share_sem.at[1, n - 1], sibling))
    for copy in root_copies:
        copy.start()
    for n in inner_chunks[1:]:
        spread_rows(n)

    @pl.when(has_up)
    def _():
        down.wait_recv()

    @pl.when(jnp.logical_not(has_up))
    def _():
        above[...] = jnp.zeros_like(above)

    @pl.when(has_down)
    def _():
        up.wait_recv()

    @pl.when(jnp.logical_not(has_down))
    def _():
        below[...] = jnp.zeros_like(below)

    for p in range(2):
        over = jnp.concatenate([above[p], x_ref[p, 0:64]], 0)
        to_flat(2, p, dot3(top, pieces(over)))
    if len(outer_chunks) == 2:
        spread_rows(outer_chunks[0])
    for p in range(2):
        under = jnp.concatenate([x_ref[p, 64:128], below[p]], 0)
        to_flat(3, p, dot3(bottom, pieces(under)))

    @pl.when(leads)
    def _():
        spread_rows(outer_chunks[-1])
        pl.semaphore_wait(ready_sem, 1)
        trans_copy.start()

    for copy in root_copies:
        copy.wait_recv()

    for ch in range(chips):
        for c in range(nc):
            one, two = roots_r[c, ch, :, 0], roots_r[c, ch, :, 1]
            at = pl.ds(2 * (nc * ch + c), 2)
            first[at], second[at] = one + two, -one * two
            gain[at] = (1.0 - one) * (1.0 - two)
    for b in range(ny):
        for n, value in enumerate(transition(roots_at(b))):
            trans[half, 4 * b + n] = value

    def back_scan(slot, begin, keep):
        def step(i, states):
            out = []
            for b, (u, t) in enumerate(states):
                at = b * block + block - 1 - i
                z = recv[slot, at] + u
                if keep:
                    recv[slot, at] = gain[at] * z
                out.append((first[at] * z + t, second[at] * z))
            return tuple(out)

        return lax.fori_loop(2, block, step, step(1, step(0, begin)))

    def fore_scan(slot, begin, keep):
        def step(k, states):
            out = []
            for b, (y1, y2) in enumerate(states):
                at = b * block + k
                y = gain[at] * recv[slot, at] + first[at] * y1 + second[at] * y2
                if keep:
                    recv[slot, at] = y
                out.append((y, y1))
            return tuple(out)

        return lax.fori_loop(2, block, step, step(1, step(0, begin)))

    zero = jnp.zeros((EIGHTHS, 128), F32)
    nothing = [(zero, zero)] * ny

    def slots(n):
        return range(CHUNKS[n][0], sum(CHUNKS[n]))

    def part(buf, n, z):
        if buf is ends:
            blocks = pl.ds(1, ny - 1) if z == 0 else pl.ds(0, ny)
        else:
            blocks = pl.ds(0, ny - 1) if z == nz - 1 else pl.ds(0, ny)
        return buf.at[pl.ds(*CHUNKS[n]), z, blocks]

    def state_sems(buf):
        return end_sem if buf is ends else end2_sem

    def far_states(buf, n, z):
        arrived(part(buf, n, 1 - z), state_sems(buf).at[1, n])

    def hand_over(buf, n, z, scan):
        for slot in slots(n):
            for b, (s1, s2) in enumerate(scan(slot, nothing, False)):
                buf[slot, z, b, 0] = s1
                buf[slot, z, b, 1] = s2
        states, sems = part(buf, n, z), state_sems(buf)
        remote(states, states, sems.at[0, n], sems.at[1, n], partner).start()

    def x_twice(slot):
        n = 2 * group * EIGHTHS
        eighth = lax.rem(lax.broadcasted_iota(jnp.int32, (n, 128), 0), EIGHTHS)
        lane = lax.broadcasted_iota(jnp.int32, (n, 128), 1)
        own = recv[slot].reshape(n, 128)
        matrix = (kx_high[...], kx_low[...])
        for _ in range(2):
            before = jnp.where(eighth == 0, 0.0, pltpu.roll(own, 1, 0))
            after = jnp.where(eighth == EIGHTHS - 1, 0.0, pltpu.roll(own, n - 1, 0))
            sides = jnp.where(lane < 64, after, before)
            own = dot3(pieces(jnp.concatenate([own, sides], 1)), matrix)
        recv[slot] = own.reshape(2 * group, EIGHTHS, 128)

    def take_in(n, z):
        arrived(recv.at[pl.ds(*CHUNKS[n]), pl.ds(0, 2 * group - 2)], in_sem.at[n])
        hand_over(ends, n, z, back_scan)

    def pass_on():
        trans_copy.wait_recv()
        for gz, _ in peers("alike"):
            remote(
                trans.at[1 - half, chip], trans.at[1 - half, chip],
                trans_sem.at[2], trans_sem.at[3], gz,
            ).start()

    def have_transitions():
        arrived(trans.at[1 - half, pl.ds(0, chips - 1)], trans_sem.at[3])

    def middle(n, mine):
        far_states(ends, n, mine)
        for slot in slots(n):
            u, t = zero, zero
            begin = [None] * ny
            for j in reversed(range(ny * nz)):
                b, z = j // nz, j % nz
                if z == mine:
                    begin[b] = (u, t)
                if j:
                    a11, a12, a21, a22 = (trans[z, 4 * b + i] for i in range(4))
                    u, t = (
                        a11 * u + a21 * t + ends[slot, z, b, 0],
                        a12 * u + a22 * t + ends[slot, z, b, 1],
                    )
            back_scan(slot, begin, True)
            x_twice(slot)
        hand_over(ends2, n, mine, fore_scan)

    def finish(n, mine):
        far_states(ends2, n, mine)
        for slot in slots(n):
            y1, y2 = zero, zero
            begin = [None] * ny
            for j in range(ny * nz):
                b, z = j // nz, j % nz
                if z == mine:
                    begin[b] = (y1, y2)
                if j < ny * nz - 1:
                    a11, a12, a21, a22 = (trans[z, 4 * b + i] for i in range(4))
                    y1, y2 = (
                        a11 * y1 + a12 * y2 + ends2[slot, z, b, 0],
                        a21 * y1 + a22 * y2 + ends2[slot, z, b, 1],
                    )
            fore_scan(slot, begin, True)
        at = pl.ds(*CHUNKS[n])
        for gz, place in peers():
            remote(
                recv.at[at, pl.ds(2 * place, 2)], back.at[at, :, flat(me)],
                home_s.at[n], home_r.at[n], gz,
            ).start()
        back[at, :, flat(me)] = recv[at, pl.ds(2 * me, 2)]

    def sent(z):
        for n in range(len(CHUNKS)):
            for buf in (ends, ends2):
                arrived(part(buf, n, z), state_sems(buf).at[0, n])

    last = len(CHUNKS)

    @pl.when(leads)
    def _():
        for n in range(last):
            take_in(n, 0)
        pass_on()
        have_transitions()
        for n in range(last):
            middle(n, 0)
            if n:
                finish(n - 1, 0)
        finish(last - 1, 0)
        sent(0)

    @pl.when(jnp.logical_not(leads))
    def _():
        take_in(0, 1)
        pass_on()
        spread_rows(outer_chunks[-1])
        take_in(1, 1)
        have_transitions()
        for n in range(2, last):
            middle(n - 2, 1)
            take_in(n, 1)
        for n in range(last - 2, last):
            middle(n, 1)
        for n in range(last):
            finish(n, 1)
        sent(1)

    for n in range(len(CHUNKS)):
        arrived(back.at[pl.ds(*CHUNKS[n]), :, pl.ds(0, (group - 1) * EIGHTHS)], home_r.at[n])
        for slot in slots(n):
            to = RUNS[slot]
            for p in range(2):
                for e in range(EIGHTHS):
                    o_ref[p, to : to + 32, 128 * e : 128 * e + 128] = back[
                        slot, p, pl.ds(e, 32, stride=EIGHTHS), :
                    ]

    @pl.when(has_up)
    def _():
        up.wait_send()

    @pl.when(has_down)
    def _():
        down.wait_send()

    trans_copy.wait_send()
    for copy in root_copies:
        copy.wait_send()
    arrived(trans.at[1 - half, pl.ds(0, chips - 1)], trans_sem.at[2])
    arrived(roots_r.at[0, pl.ds(0, nxx * nc - 1)], row_sem.at[0])
    arrived(roots_r.at[0, pl.ds(0, chips - nxx)], root_sem.at[0])
    for n in range(len(CHUNKS)):
        at = pl.ds(*CHUNKS[n])
        arrived(send.at[at, :, pl.ds(0, (group - 1) * EIGHTHS)], out_sem.at[n])
        arrived(back.at[at, :, pl.ds(0, (group - 1) * EIGHTHS)], home_s.at[n])


def build(sizes, n_slabs):
    ny, nz, nxx, nc = sizes
    chips = ny * nxx
    group = chips * nc
    steps = len(CHUNKS)

    def body(probe_fields, root_one, root_two, lateral_kernel_taps, dilations):
        dma, vmem, smem = pltpu.SemaphoreType.DMA, pltpu.VMEM, pltpu.SMEM
        out = pl.pallas_call(
            functools.partial(kernel, sizes, n_slabs),
            out_shape=jax.ShapeDtypeStruct((2, 128, 1024), F32),
            in_specs=[pl.BlockSpec(memory_space=pltpu.HBM)] * 5,
            out_specs=pl.BlockSpec(memory_space=vmem),
            scratch_shapes=[
                vmem((2, 128, 1024), F32),
                vmem((2, 1024), F32),
                vmem((2, 1024), F32),
                smem((2, 3), F32),
                smem((2,), jnp.int32),
                vmem((4, 2, 256, 128), F32),
                vmem((4, 2 * group, 8, 128), F32),
                vmem((4, 2, 256, 128), F32),
                vmem((2, 2, 8, 128), F32),
                vmem((nc, chips, 2, 2, 8, 128), F32),
                vmem((2 * group, 8, 128), F32),
                vmem((2 * group, 8, 128), F32),
                vmem((2 * group, 8, 128), F32),
                vmem((2, 32, 1024), F32),
                vmem((2, 32, 1024), F32),
                vmem((256, 128), BF16),
                vmem((256, 128), BF16),
                vmem((4, 8, 128), F32),
                vmem((nz, 4 * ny, 8, 128), F32),
                vmem((4, nz, ny, 2, 8, 128), F32),
                vmem((4, nz, ny, 2, 8, 128), F32),
                dma((5,)),
                pltpu.SemaphoreType.REGULAR,
                dma((2,)),
                dma((2,)),
                dma((2, ny - 1)),
                dma((4,)),
                dma((steps,)),
                dma((steps,)),
                dma((4,)),
                dma((2, steps)),
                dma((2, steps)),
                dma((steps,)),
                dma((steps,)),
            ],
            compiler_params=pltpu.CompilerParams(
                collective_id=0, has_side_effects=True, vmem_limit_bytes=48 << 20
            ),
        )(
            *(
                pltpu.with_memory_space_constraint(a, pltpu.HBM)
                for a in (probe_fields[0], root_one, root_two, lateral_kernel_taps, dilations)
            )
        )
        return out[None]

    return body


def solution(mesh):
    placed = (P(None, "gz", "gy", None), P("gz", None), P("gz", None), P(), P())
    return jax.shard_map(
        build(SIZES, mesh.shape["gy"]),
        mesh=mesh,
        in_specs=placed,
        out_specs=P(None, "gz", "gy", None),
        check_vma=False,
    )
```

```python
import functools
import jax
import jax.numpy as jnp
from jax import lax
from jax.experimental import pallas as pl
from jax.experimental.pallas import tpu as pltpu
from jax.sharding import PartitionSpec as P

MESH = pl.DeviceIdType.MESH
F32 = jnp.float32
BF16 = jnp.bfloat16
SIZES = (4, 2, 4, 2)
MARGIN = 16
EIGHTHS = 8
RUNS = (32, 64, 0, 96)
CHUNKS = ((0, 1), (1, 1), (2, 1), (3, 1))


def pieces(a):
    high = a.astype(BF16)
    return high, (a - high.astype(F32)).astype(BF16)


def dot3(a, b):
    (ah, al), (bh, bl) = a, b
    dot = functools.partial(jnp.dot, preferred_element_type=F32)
    return dot(ah, bh) + (dot(ah, bl) + dot(al, bh))


def stencil(away, taps, row, step):
    centre, near, far = taps[row, 0], taps[row, 1], taps[row, 2]
    weight = jnp.where(away == 0, centre, 0.0)
    weight = jnp.where(away == step, near, weight)
    weight = jnp.where(away == 2 * step, far, weight)
    return weight / (centre + 2.0 * (near + far))


def kernel(
    sizes, n_slabs, x_hbm, one_hbm, two_hbm, taps_hbm, dils_hbm, o_ref,
    x_ref, one_ref, two_ref, taps, dils, send, recv, back, roots_s, roots_r, first, second, gain,
    above, below, kx_both, entry, trans, ends, ends2,
    load_sem, ready_sem, row_sem, root_sem, share_sem, halo_sem, out_sem, in_sem, trans_sem, end_sem, end2_sem, home_s, home_r,
):
    ny, nz, nxx, nc = sizes
    chips = ny * nxx
    group = chips * nc
    block = nxx * nc * 2
    g, gy = lax.axis_index("gz"), lax.axis_index("gy")
    core, col = lax.rem(g, nc), lax.rem(g // nc, nxx)
    half, line = lax.rem(g // (nc * nxx), nz), g // (nc * nxx * nz)
    chip = line * nxx + col
    me = chip * nc + core

    def gz_of(yy, zz, xx, cc):
        return ((yy * nz + zz) * nxx + xx) * nc + cc

    partner, sibling = gz_of(line, 1 - half, col, core), gz_of(line, half, col, 1 - core)

    def reach(n, step):
        return min(step, n - step)

    steps = [(a, b, c) for a in range(ny) for b in range(nxx) for c in range(nc)][1:]
    steps.sort(key=lambda s: (-reach(ny, s[0]) - reach(nxx, s[1]), -min(s[0], 1) - min(s[1], 1)))

    def peers(kind="all"):
        for a, b, c in steps:
            if not {"all": True, "row": a == 0, "core": a and not c, "alike": not c}[kind]:
                continue
            yy, xx, cc = lax.rem(line + a, ny), lax.rem(col + b, nxx), lax.rem(core + c, nc)
            yield gz_of(yy, half, xx, cc), (yy * nxx + xx) * nc + cc

    def remote(src, dst, s, r, gz, slab=gy):
        return pltpu.make_async_remote_copy(
            src, dst, s, r, device_id=(gz, slab), device_id_type=MESH
        )

    def arrived(ref, sem):
        pltpu.make_async_copy(ref, ref, sem).wait()

    def flat(place):
        return pl.ds(pl.multiple_of(place * EIGHTHS, EIGHTHS), EIGHTHS)

    loads = [
        pltpu.make_async_copy(a, b, load_sem.at[i])
        for i, (a, b) in enumerate(
            (
                (one_hbm, one_ref),
                (two_hbm, two_ref),
                (taps_hbm, taps),
                (dils_hbm, dils),
                (x_hbm, x_ref),
            )
        )
    ]
    for copy in loads:
        copy.start()

    has_up, has_down = gy > 0, gy < n_slabs - 1

    barrier = pltpu.get_barrier_semaphore()

    def hello(gz, slab):
        pl.semaphore_signal(barrier, inc=1, device_id=(gz, slab), device_id_type=MESH)

    leads = half == 0

    @pl.when(leads)
    def _():
        hello(partner, gy)

    @pl.when(has_up)
    def _():
        hello(g, gy - 1)

    @pl.when(has_down)
    def _():
        hello(g, gy + 1)

    for gz, _ in peers():
        hello(gz, gy)

    loads[0].wait()
    loads[1].wait()
    for p in range(2):
        for e in range(EIGHTHS):
            lanes = slice(128 * e, 128 * e + 128)
            roots_s[p, 0, e : e + 1, :] = one_ref[p : p + 1, lanes]
            roots_s[p, 1, e : e + 1, :] = two_ref[p : p + 1, lanes]

    loads[2].wait()
    loads[3].wait()
    exact = functools.partial(jnp.dot, precision=lax.Precision.HIGHEST, preferred_element_type=F32)

    def ky(n_out, n_in):
        i = lax.broadcasted_iota(jnp.int32, (n_out, n_in), 0)
        j = lax.broadcasted_iota(jnp.int32, (n_out, n_in), 1)
        return stencil(jnp.abs(i - j + MARGIN), taps, 1, dils[1])

    def to_flat(slot, p, value):
        for e in range(EIGHTHS):
            send[slot, p, pl.ds(e, 32, stride=EIGHTHS), :] = value[:, 128 * e : 128 * e + 128]

    inner = pieces(exact(ky(64, 96), ky(96, 128)))
    loads[4].wait()
    for p in range(2):
        middle = dot3(inner, pieces(x_ref[p]))
        to_flat(0, p, middle[:32])
        to_flat(1, p, middle[32:])

    pl.semaphore_wait(
        barrier, group - 1 + half + has_up.astype(jnp.int32) + has_down.astype(jnp.int32)
    )

    @pl.when(jnp.logical_not(leads))
    def _():
        pl.semaphore_signal(ready_sem, inc=1, device_id=(partner, gy), device_id_type=MESH)

    for gz, _ in peers("row"):
        remote(roots_s, roots_r.at[core, chip], row_sem.at[0], row_sem.at[1], gz).start()
    for gz, _ in peers("core"):
        remote(roots_s, roots_r.at[core, chip], root_sem.at[0], root_sem.at[1], gz).start()
    roots_r[core, chip] = roots_s[...]
    up = remote(x_ref.at[:, 0:32], below, halo_sem.at[0], halo_sem.at[2], g, gy - 1)
    down = remote(x_ref.at[:, 96:128], above, halo_sem.at[1], halo_sem.at[3], g, gy + 1)

    @pl.when(has_up)
    def _():
        up.start()

    @pl.when(has_down)
    def _():
        down.start()

    def spread_rows(n):
        at = pl.ds(*CHUNKS[n])
        for gz, place in peers():
            remote(
                send.at[at, :, flat(place)], recv.at[at, pl.ds(2 * me, 2)],
                out_sem.at[n], in_sem.at[n], gz,
            ).start()
        recv[at, pl.ds(2 * me, 2)] = send[at, :, flat(me)]

    inner_chunks = [n for n, (s, _) in enumerate(CHUNKS) if s < 2]
    outer_chunks = [n for n, (s, _) in enumerate(CHUNKS) if s >= 2]
    spread_rows(inner_chunks[0])

    i = lax.broadcasted_iota(jnp.int32, (256, 128), 0)
    j = lax.broadcasted_iota(jnp.int32, (256, 128), 1)
    kx = stencil(jnp.abs(jnp.where(i < 192, i, i - 256) - j), taps, 0, dils[0])
    kx_both[:, :128], kx_both[:, 128:] = pieces(kx)

    head, tail = ky(32, 64), ky(64, 96)
    mid = lax.broadcasted_iota(jnp.int32, (64, 96), 0)
    top = pieces(exact(head, jnp.where(has_up | (mid >= MARGIN), tail, 0.0)))
    bottom = pieces(exact(head, jnp.where(has_down | (mid < 64 - MARGIN), tail, 0.0)))

    def transition(roots_of):
        (f0, s0), (f, s) = (
            (one + two, -one * two) for one, two in (roots_of(0), roots_of(1))
        )
        y = [(f * f0 + s, f0), (f * s0, s0)]
        for k in range(2, block):
            one, two = roots_of(k)
            f, s = one + two, -one * two
            y = [(f * y1 + s * y2, y1) for y1, y2 in y]
        (a, c), (d, e) = y
        return a, d, c, e

    def roots_at(row):
        def of(k):
            c, ch, p = k // 2 % nc, row * nxx + k // (2 * nc), k % 2
            return roots_r[c, ch, p, 0], roots_r[c, ch, p, 1]

        return of

    arrived(roots_r.at[0, pl.ds(0, nxx * nc - 1)], row_sem.at[1])
    for n, value in enumerate(transition(roots_at(line))):
        entry[n] = value
    trans_copy = remote(
        entry.at[col], trans.at[half, chip], trans_sem.at[0], trans_sem.at[1], partner
    )

    @pl.when(jnp.logical_not(leads))
    def _():
        trans_copy.start()

    arrived(roots_r.at[0, pl.ds(0, chips - nxx)], root_sem.at[1])
    root_copies = []
    for n in range(1, ny):
        other = roots_r.at[core, pl.ds(lax.rem(line + n, ny) * nxx, nxx)]
        root_copies.append(remote(other, other, share_sem.at[0, n - 1], share_sem.at[1, n - 1], sibling))
    for copy in root_copies:
        copy.start()
    for n in inner_chunks[1:]:
        spread_rows(n)

    @pl.when(has_up)
    def _():
        down.wait_recv()

    @pl.when(jnp.logical_not(has_up))
    def _():
        above[...] = jnp.zeros_like(above)

    @pl.when(has_down)
    def _():
        up.wait_recv()

    @pl.when(jnp.logical_not(has_down))
    def _():
        below[...] = jnp.zeros_like(below)

    for p in range(2):
        over = jnp.concatenate([above[p], x_ref[p, 0:64]], 0)
        to_flat(2, p, dot3(top, pieces(over)))
    if len(outer_chunks) == 2:
        spread_rows(outer_chunks[0])
    for p in range(2):
        under = jnp.concatenate([x_ref[p, 64:128], below[p]], 0)
        to_flat(3, p, dot3(bottom, pieces(under)))

    @pl.when(leads)
    def _():
        spread_rows(outer_chunks[-1])
        pl.semaphore_wait(ready_sem, 1)
        trans_copy.start()

    for copy in root_copies:
        copy.wait_recv()

    for ch in range(chips):
        for c in range(nc):
            one, two = roots_r[c, ch, :, 0], roots_r[c, ch, :, 1]
            at = pl.ds(2 * (nc * ch + c), 2)
            first[at], second[at] = one + two, -one * two
            gain[at] = (1.0 - one) * (1.0 - two)
    for b in range(ny):
        for n, value in enumerate(transition(roots_at(b))):
            trans[half, 4 * b + n] = value

    def back_scan(slot, begin, keep):
        def step(i, states):
            out = []
            for b, (u, t) in enumerate(states):
                at = b * block + block - 1 - i
                z = recv[slot, at] + u
                if keep:
                    recv[slot, at] = gain[at] * z
                out.append((first[at] * z + t, second[at] * z))
            return tuple(out)

        return lax.fori_loop(2, block, step, step(1, step(0, begin)))

    def fore_scan(slot, begin, keep):
        def step(k, states):
            out = []
            for b, (y1, y2) in enumerate(states):
                at = b * block + k
                y = gain[at] * recv[slot, at] + first[at] * y1 + second[at] * y2
                if keep:
                    recv[slot, at] = y
                out.append((y, y1))
            return tuple(out)

        return lax.fori_loop(2, block, step, step(1, step(0, begin)))

    zero = jnp.zeros((EIGHTHS, 128), F32)
    nothing = [(zero, zero)] * ny

    def slots(n):
        return range(CHUNKS[n][0], sum(CHUNKS[n]))

    def part(buf, n, z):
        if buf is ends:
            blocks = pl.ds(1, ny - 1) if z == 0 else pl.ds(0, ny)
        else:
            blocks = pl.ds(0, ny - 1) if z == nz - 1 else pl.ds(0, ny)
        return buf.at[pl.ds(*CHUNKS[n]), z, blocks]

    def state_sems(buf):
        return end_sem if buf is ends else end2_sem

    def far_states(buf, n, z):
        arrived(part(buf, n, 1 - z), state_sems(buf).at[1, n])

    def hand_over(buf, n, z, scan):
        for slot in slots(n):
            for b, (s1, s2) in enumerate(scan(slot, nothing, False)):
                buf[slot, z, b, 0] = s1
                buf[slot, z, b, 1] = s2
        states, sems = part(buf, n, z), state_sems(buf)
        remote(states, states, sems.at[0, n], sems.at[1, n], partner).start()

    def x_twice(slot):
        n = 2 * group
        eighth = lax.broadcasted_iota(jnp.int32, (n, EIGHTHS, 128), 1)
        lane = lax.broadcasted_iota(jnp.int32, (n, EIGHTHS, 128), 2)
        own = recv[slot]
        for _ in range(2):
            before = jnp.where(eighth == 0, 0.0, pltpu.roll(own, 1, 1))
            after = jnp.where(eighth == EIGHTHS - 1, 0.0, pltpu.roll(own, EIGHTHS - 1, 1))
            sides = jnp.where(lane < 64, after, before)
            both = jnp.concatenate([own, sides], 2).reshape(n * EIGHTHS, 256)
            high, low = pieces(both)
            wide = jnp.dot(high, kx_both[...], preferred_element_type=F32)
            rest = jnp.dot(low, kx_both[:, :128], preferred_element_type=F32)
            own = (wide[:, :128] + (wide[:, 128:] + rest)).reshape(n, EIGHTHS, 128)
        recv[slot] = own

    def take_in(n, z):
        arrived(recv.at[pl.ds(*CHUNKS[n]), pl.ds(0, 2 * group - 2)], in_sem.at[n])
        hand_over(ends, n, z, back_scan)

    def pass_on():
        trans_copy.wait_recv()
        for gz, _ in peers("alike"):
            remote(
                trans.at[1 - half, chip], trans.at[1 - half, chip],
                trans_sem.at[2], trans_sem.at[3], gz,
            ).start()

    def have_transitions():
        arrived(trans.at[1 - half, pl.ds(0, chips - 1)], trans_sem.at[3])

    def middle(n, mine):
        far_states(ends, n, mine)
        for slot in slots(n):
            u, t = zero, zero
            begin = [None] * ny
            for j in reversed(range(ny * nz)):
                b, z = j // nz, j % nz
                if z == mine:
                    begin[b] = (u, t)
                if j:
                    a11, a12, a21, a22 = (trans[z, 4 * b + i] for i in range(4))
                    u, t = (
                        a11 * u + a21 * t + ends[slot, z, b, 0],
                        a12 * u + a22 * t + ends[slot, z, b, 1],
                    )
            back_scan(slot, begin, True)
            x_twice(slot)
        hand_over(ends2, n, mine, fore_scan)

    def finish(n, mine):
        far_states(ends2, n, mine)
        for slot in slots(n):
            y1, y2 = zero, zero
            begin = [None] * ny
            for j in range(ny * nz):
                b, z = j // nz, j % nz
                if z == mine:
                    begin[b] = (y1, y2)
                if j < ny * nz - 1:
                    a11, a12, a21, a22 = (trans[z, 4 * b + i] for i in range(4))
                    y1, y2 = (
                        a11 * y1 + a12 * y2 + ends2[slot, z, b, 0],
                        a21 * y1 + a22 * y2 + ends2[slot, z, b, 1],
                    )
            fore_scan(slot, begin, True)
        at = pl.ds(*CHUNKS[n])
        for gz, place in peers():
            remote(
                recv.at[at, pl.ds(2 * place, 2)], back.at[at, :, flat(me)],
                home_s.at[n], home_r.at[n], gz,
            ).start()
        back[at, :, flat(me)] = recv[at, pl.ds(2 * me, 2)]

    def sent(z):
        for n in range(len(CHUNKS)):
            for buf in (ends, ends2):
                arrived(part(buf, n, z), state_sems(buf).at[0, n])

    last = len(CHUNKS)

    @pl.when(leads)
    def _():
        for n in range(last):
            take_in(n, 0)
        pass_on()
        have_transitions()
        for n in range(last):
            middle(n, 0)
            if n:
                finish(n - 1, 0)
        finish(last - 1, 0)
        sent(0)

    @pl.when(jnp.logical_not(leads))
    def _():
        take_in(0, 1)
        pass_on()
        spread_rows(outer_chunks[-1])
        take_in(1, 1)
        have_transitions()
        for n in range(2, last):
            middle(n - 2, 1)
            take_in(n, 1)
        for n in range(last - 2, last):
            middle(n, 1)
        for n in range(last):
            finish(n, 1)
        sent(1)

    for n in range(len(CHUNKS)):
        arrived(back.at[pl.ds(*CHUNKS[n]), :, pl.ds(0, (group - 1) * EIGHTHS)], home_r.at[n])
        for slot in slots(n):
            to = RUNS[slot]
            for p in range(2):
                for e in range(EIGHTHS):
                    o_ref[p, to : to + 32, 128 * e : 128 * e + 128] = back[
                        slot, p, pl.ds(e, 32, stride=EIGHTHS), :
                    ]

    @pl.when(has_up)
    def _():
        up.wait_send()

    @pl.when(has_down)
    def _():
        down.wait_send()

    trans_copy.wait_send()
    for copy in root_copies:
        copy.wait_send()
    arrived(trans.at[1 - half, pl.ds(0, chips - 1)], trans_sem.at[2])
    arrived(roots_r.at[0, pl.ds(0, nxx * nc - 1)], row_sem.at[0])
    arrived(roots_r.at[0, pl.ds(0, chips - nxx)], root_sem.at[0])
    for n in range(len(CHUNKS)):
        at = pl.ds(*CHUNKS[n])
        arrived(send.at[at, :, pl.ds(0, (group - 1) * EIGHTHS)], out_sem.at[n])
        arrived(back.at[at, :, pl.ds(0, (group - 1) * EIGHTHS)], home_s.at[n])


def build(sizes, n_slabs):
    ny, nz, nxx, nc = sizes
    chips = ny * nxx
    group = chips * nc
    steps = len(CHUNKS)

    def body(probe_fields, root_one, root_two, lateral_kernel_taps, dilations):
        dma, vmem, smem = pltpu.SemaphoreType.DMA, pltpu.VMEM, pltpu.SMEM
        out = pl.pallas_call(
            functools.partial(kernel, sizes, n_slabs),
            out_shape=jax.ShapeDtypeStruct((2, 128, 1024), F32),
            in_specs=[pl.BlockSpec(memory_space=pltpu.HBM)] * 5,
            out_specs=pl.BlockSpec(memory_space=vmem),
            scratch_shapes=[
                vmem((2, 128, 1024), F32),
                vmem((2, 1024), F32),
                vmem((2, 1024), F32),
                smem((2, 3), F32),
                smem((2,), jnp.int32),
                vmem((4, 2, 256, 128), F32),
                vmem((4, 2 * group, 8, 128), F32),
                vmem((4, 2, 256, 128), F32),
                vmem((2, 2, 8, 128), F32),
                vmem((nc, chips, 2, 2, 8, 128), F32),
                vmem((2 * group, 8, 128), F32),
                vmem((2 * group, 8, 128), F32),
                vmem((2 * group, 8, 128), F32),
                vmem((2, 32, 1024), F32),
                vmem((2, 32, 1024), F32),
                vmem((256, 256), BF16),
                vmem((4, 8, 128), F32),
                vmem((nz, 4 * ny, 8, 128), F32),
                vmem((4, nz, ny, 2, 8, 128), F32),
                vmem((4, nz, ny, 2, 8, 128), F32),
                dma((5,)),
                pltpu.SemaphoreType.REGULAR,
                dma((2,)),
                dma((2,)),
                dma((2, ny - 1)),
                dma((4,)),
                dma((steps,)),
                dma((steps,)),
                dma((4,)),
                dma((2, steps)),
                dma((2, steps)),
                dma((steps,)),
                dma((steps,)),
            ],
            compiler_params=pltpu.CompilerParams(
                collective_id=0, has_side_effects=True, vmem_limit_bytes=48 << 20
            ),
        )(
            *(
                pltpu.with_memory_space_constraint(a, pltpu.HBM)
                for a in (probe_fields[0], root_one, root_two, lateral_kernel_taps, dilations)
            )
        )
        return out[None]

    return body


def solution(mesh):
    placed = (P(None, "gz", "gy", None), P("gz", None), P("gz", None), P(), P())
    return jax.shard_map(
        build(SIZES, mesh.shape["gy"]),
        mesh=mesh,
        in_specs=placed,
        out_specs=P(None, "gz", "gy", None),
        check_vma=False,
    )
```
